256 devices in a mesh: dp: 16 (over y, x), tile: 16 (over z, core).
Axes of the slice: x: 4, y: 4, z: 8, core: 2. Of those that a mesh axis runs over, the one named last changes fastest.
Arguments:
- tokens: bfloat16 [2048, 4096], P('dp', 'tile'), may hold values from -6 to 6
- grad_out: bfloat16 [2048, 4096], P('dp', 'tile'), may hold values from -6 to 6
- up_tiles: bfloat16 [16, 128, 128, 128], P('tile'), may hold values from -0.1875 to 0.1875
- down_tiles: bfloat16 [16, 128, 128, 128], P('tile'), may hold values from -0.09375 to 0.09375
- tile_rows: int32 [16, 128], P('tile'), may hold values from 0 to 7, as said below
- tile_cols: int32 [16, 128], P('tile'), may hold values from 0 to 31
- tile_count: int32 [16], P('tile'), may hold values from 16 to 128, as said below
Outputs:
- mixed: bfloat16 [2048, 4096], P('dp', 'tile')
- grad_in: bfloat16 [2048, 4096], P('dp', 'tile')
- grad_up: float32 [16, 128, 128, 128], P('tile', 'dp')
- grad_down: float32 [16, 128, 128, 128], P('tile', 'dp')
The draws below stay inside these ranges and needn't reach their ends.
Inputs may be any that keep to these rules, and one draw needn't show every extreme that they name: `tile_count`: some owner holds exactly 128 tiles in every draw. The pairs (tile_rows[i, s], tile_cols[i, s]) of one owner are distinct over all its 128 slots.
All inputs are finite; a program needn't handle non-finite values.
Results may differ from the reference program's by a relative error of at most 0.015.
Values may be sent and summed in bfloat16 or wider, within the bound.
No kernel may reach another device: no remote copies, remote signals or barrier semaphores. Data moves between devices by JAX's collectives and lax.ppermute only.
A program may use at most 128 MiB of HBM per device.

```python
import jax
import jax.numpy as jnp
from jax import lax

D = 4096
HIDDEN_SIZE = 16384
TILE = 128
TOK_DEV = 128
TOKENS = 2048
COLS = 32
ROWS_DEV = 8
CAP = 128
N_DP = 16
N_TILE = 16


def make_pattern(key):
    base = jax.random.fold_in(key, 271)
    key_heavy, key_counts, key_slots = jax.random.split(jax.random.fold_in(base, 5), 3)
    heavy = jax.random.randint(key_heavy, (), 0, N_TILE)
    counts = jax.random.randint(key_counts, (N_TILE,), CAP // 8, CAP // 2 + 1)
    counts = jnp.where(jnp.arange(N_TILE) == heavy, CAP, counts).astype(jnp.int32)
    cells = ROWS_DEV * COLS

    def owner_slots(dev_key, count):
        key_level, key_noise, key_shuffle = jax.random.split(dev_key, 3)
        level = jax.random.randint(key_level, (ROWS_DEV, 1), 0, 4)
        noise = jax.random.randint(key_noise, (ROWS_DEV, COLS), 0, 4096)
        score = (level * 4096 + noise).reshape(cells) * cells + jnp.arange(cells, dtype=jnp.int32)
        chosen = jnp.argsort(-score)[:CAP]
        slot = jnp.arange(CAP, dtype=jnp.int32)
        shuffle = jax.random.randint(key_shuffle, (CAP,), 0, 4096)
        ranking = jnp.where(slot < count, 0, 1) * (4096 * CAP) + shuffle * CAP + slot
        chosen = chosen[jnp.argsort(ranking)]
        return ((chosen // COLS).astype(jnp.int32), (chosen % COLS).astype(jnp.int32))
    rows, cols = jax.vmap(owner_slots)(jax.random.split(key_slots, N_TILE), counts)
    return (rows, cols, counts)


def draw_tile_rows(key, part):
    return make_pattern(key)[0]


def draw_tile_cols(key, part):
    return make_pattern(key)[1]


def draw_tile_count(key, part):
    return make_pattern(key)[2]


def block_scale(key, dims, cuts, low, top_value):
    loudness, own = 1.0, jax.random.fold_in(key, 6)
    for dim, blocks in cuts:
        heights = jnp.exp(jax.random.uniform(jax.random.fold_in(own, dim), (blocks,), jnp.float32, low / len(cuts), top_value / len(cuts)))
        loudness = loudness * jnp.repeat(heights, dims[dim] // blocks).reshape([-1 if axis == dim else 1 for axis in range(len(dims))])
    return loudness


def scatter_about(key, shape, scale, reach, cuts=(), kind=jnp.bfloat16):
    entries = scale * jax.random.normal(key, shape, jnp.float32)
    if cuts:
        entries = entries * block_scale(key, shape, cuts, -0.22, 0.18)
    return jnp.clip(entries, -reach, reach).astype(kind)


def setup_inputs(seed: int = 0) -> dict:
    seeds = jax.random.split(jax.random.key(seed), 8)
    return {
        "tokens": scatter_about(seeds[0], (TOKENS, D), 1.0, 6.0, ((0, 16), (1, 16))),
        "grad_out": scatter_about(seeds[1], (TOKENS, D), 1.0, 6.0, ((0, 16), (1, 16))),
        "up_tiles": scatter_about(seeds[2], (N_TILE, CAP, TILE, TILE), (D // 4) ** -0.5, 0.1875, ((0, 16),)),
        "down_tiles": scatter_about(seeds[3], (N_TILE, CAP, TILE, TILE), (HIDDEN_SIZE // 4) ** -0.5, 0.09375, ((0, 16),)),
        "tile_rows": draw_tile_rows(jax.random.fold_in(seeds[7], 71), 0),
        "tile_cols": draw_tile_cols(jax.random.fold_in(seeds[7], 71), 0),
        "tile_count": draw_tile_count(jax.random.fold_in(seeds[7], 71), 0),
    }


def gelu_pair(pre):
    curve = jax.scipy.special.erf(pre * 0.7071067811865476)
    value = 0.5 * pre * (1.0 + curve)
    slope = 0.5 * (1.0 + curve) + pre * jnp.exp(-0.5 * pre * pre) * 0.3989422804014327
    return value, slope


def add_owner(total, pair):
    part = jnp.dot(pair[0], pair[1], preferred_element_type=jnp.float32)
    rounded = lax.optimization_barrier(part.astype(jnp.bfloat16))
    return total + rounded.astype(jnp.float32), None


def add_group(totals, group):
    x_group, dy_group, h_group, d_group = group
    up_part = jnp.dot(x_group.T, d_group, preferred_element_type=jnp.float32)
    down_part = jnp.dot(h_group.T, dy_group, preferred_element_type=jnp.float32)
    up_round = lax.optimization_barrier(up_part.astype(jnp.bfloat16))
    down_round = lax.optimization_barrier(down_part.astype(jnp.bfloat16))
    return (totals[0] + up_round.astype(jnp.float32), totals[1] + down_round.astype(jnp.float32)), None


def reference(tokens, grad_out, up_tiles, down_tiles, tile_rows, tile_cols, tile_count):
    hrows = HIDDEN_SIZE // TILE
    width = ROWS_DEV * TILE
    valid = jnp.arange(CAP, dtype=jnp.int32)[None, :] < tile_count[:, None]
    keep = valid.astype(up_tiles.dtype)
    grow = (tile_rows + ROWS_DEV * jnp.arange(N_TILE, dtype=jnp.int32)[:, None]).reshape(-1)
    gcol = tile_cols.reshape(-1)
    up_live = (up_tiles * keep[:, :, None, None]).reshape(N_TILE * CAP, TILE, TILE)
    down_live = (down_tiles * keep[:, :, None, None]).reshape(N_TILE * CAP, TILE, TILE)
    up_dense = jnp.zeros((COLS, TILE, hrows, TILE), up_tiles.dtype).at[gcol, :, grow, :].add(up_live).reshape(D, HIDDEN_SIZE)
    down_dense = jnp.zeros((hrows, TILE, COLS, TILE), down_tiles.dtype).at[grow, :, gcol, :].add(down_live).reshape(HIDDEN_SIZE, D)
    pre = jnp.dot(tokens, up_dense, preferred_element_type=jnp.float32)
    value, slope = gelu_pair(pre)
    hidden = value.astype(jnp.bfloat16)
    h_blocks = hidden.reshape(TOKENS, N_TILE, width).transpose(1, 0, 2)
    down_blocks = down_dense.reshape(N_TILE, width, D)
    mixed_total, _ = lax.scan(add_owner, jnp.zeros((TOKENS, D), jnp.float32), (h_blocks, down_blocks))
    mixed = mixed_total.astype(jnp.bfloat16)
    grad_hidden = jnp.dot(grad_out, down_dense.T, preferred_element_type=jnp.float32)
    grad_pre = (grad_hidden * slope).astype(jnp.bfloat16)
    d_blocks = grad_pre.reshape(TOKENS, N_TILE, width).transpose(1, 0, 2)
    up_blocks = up_dense.reshape(D, N_TILE, width).transpose(1, 2, 0)
    input_total, _ = lax.scan(add_owner, jnp.zeros((TOKENS, D), jnp.float32), (d_blocks, up_blocks))
    grad_in = input_total.astype(jnp.bfloat16)
    groups = (tokens.reshape(N_DP, TOK_DEV, D), grad_out.reshape(N_DP, TOK_DEV, D),
              hidden.reshape(N_DP, TOK_DEV, HIDDEN_SIZE), grad_pre.reshape(N_DP, TOK_DEV, HIDDEN_SIZE))
    start = (jnp.zeros((D, HIDDEN_SIZE), jnp.float32), jnp.zeros((HIDDEN_SIZE, D), jnp.float32))
    (up_sum, down_sum), _ = lax.scan(add_group, start, groups)
    up_sum = up_sum * (1.0 / N_DP)
    down_sum = down_sum * (1.0 / N_DP)
    live = valid.astype(jnp.float32)[:, :, None, None]
    grad_up = up_sum.reshape(COLS, TILE, hrows, TILE)[gcol, :, grow, :].reshape(N_TILE, CAP, TILE, TILE) * live
    grad_down = down_sum.reshape(hrows, TILE, COLS, TILE)[grow, :, gcol, :].reshape(N_TILE, CAP, TILE, TILE) * live
    return mixed, grad_in, grad_up, grad_down
```

```python
import functools

import jax
import jax.numpy as jnp
from jax import lax
from jax.experimental import pallas as pl
from jax.experimental.pallas import tpu as pltpu
from jax.sharding import Mesh, PartitionSpec as P

SIDE = 128
COLS = 32
ROWS = 8
SLOTS = 128
GROUP = 16
STEPS = SLOTS // GROUP
VM = pltpu.VMEM
SM = pltpu.SMEM
BF = jnp.bfloat16
F32 = jnp.float32


def vspec():
    return pl.BlockSpec(memory_space=VM)


def sspec():
    return pl.BlockSpec(memory_space=SM)


def nn(a, b):
    return jnp.dot(a, b, preferred_element_type=F32)


def nt(a, b):
    return lax.dot_general(a, b, (((1,), (1,)), ((), ())), preferred_element_type=F32)


def gelu_pair(pre):
    curve = lax.erf(pre * 0.7071067811865476)
    value = 0.5 * pre * (1.0 + curve)
    slope = 0.5 * (1.0 + curve) + pre * jnp.exp(-0.5 * pre * pre) * 0.3989422804014327
    return value, slope


def forward_kernel(rows, cols, meta, owners, *refs):
    shards = refs[:16]
    up_ref, down_ref = refs[16:18]
    x_ref, dy_ref, h_ref, ht_ref, d_ref, dt_ref = refs[18:24]
    pre_acc, gh_acc = refs[24:26]
    step = pl.program_id(0)
    count = meta[0]

    @pl.when(step == 0)
    def _():
        pre_acc[...] = jnp.zeros_like(pre_acc)
        gh_acc[...] = jnp.zeros_like(gh_acc)
        for k in range(16):
            at = owners[k] * 2
            for b in range(2):
                x_ref[at + b] = shards[k][0, :, b * SIDE : (b + 1) * SIDE]
                dy_ref[at + b] = shards[k][1, :, b * SIDE : (b + 1) * SIDE]

    for s in range(GROUP):
        slot = step * GROUP + s
        live = slot < count
        r = rows[slot]
        c = cols[slot]
        up = up_ref[0, s]
        down = down_ref[0, s]
        up = jnp.where(live, up, jnp.zeros_like(up))
        down = jnp.where(live, down, jnp.zeros_like(down))
        pre_acc[r] += nn(x_ref[c], up)
        gh_acc[r] += nt(dy_ref[c], down)

    @pl.when(step == STEPS - 1)
    def _():
        for r in range(ROWS):
            value, slope = gelu_pair(pre_acc[r])
            grad = gh_acc[r] * slope
            h_ref[r] = value.astype(BF)
            ht_ref[r] = value.T.astype(BF)
            d_ref[r] = grad.astype(BF)
            dt_ref[r] = grad.T.astype(BF)


def forward(rows, cols, meta, owners, shards, up_tiles, down_tiles):
    block = pl.BlockSpec((1, GROUP, SIDE, SIDE), lambda i: (0, i, 0, 0))
    tok = jax.ShapeDtypeStruct((COLS, SIDE, SIDE), BF)
    hid = jax.ShapeDtypeStruct((ROWS, SIDE, SIDE), BF)
    return pl.pallas_call(
        forward_kernel,
        grid=(STEPS,),
        in_specs=[sspec()] * 4 + [vspec()] * 16 + [block] * 2,
        out_specs=[vspec()] * 6,
        out_shape=[tok, tok, hid, hid, hid, hid],
        scratch_shapes=[VM((ROWS, SIDE, SIDE), F32)] * 2,
        compiler_params=pltpu.CompilerParams(vmem_limit_bytes=24 << 20),
        cost_estimate=pl.CostEstimate(flops=1 << 30, bytes_accessed=12 << 20, transcendentals=1 << 18),
        name="forward",
    )(rows, cols, meta, owners, *shards, up_tiles, down_tiles)


def weight_kernel(n, rows, cols, up_slots, down_slots, x_ref, dy_ref, ht_ref, dt_ref, *outs):
    half = len(outs) // 2
    for k in range(half):
        for s in range(n):
            slot = up_slots[k * n + s]
            outs[k][s] = nn(dt_ref[rows[slot]], x_ref[cols[slot]]).astype(BF)
            slot = down_slots[k * n + s]
            outs[half + k][s] = nn(ht_ref[rows[slot]], dy_ref[cols[slot]]).astype(BF)


def weight_parts(rows, cols, up_slots, down_slots, x, dy, ht, dt, n):
    k = up_slots.shape[0] // n
    part = jax.ShapeDtypeStruct((n, SIDE, SIDE), BF)
    outs = pl.pallas_call(
        functools.partial(weight_kernel, n),
        in_specs=[sspec()] * 4 + [vspec()] * 4,
        out_specs=[vspec()] * (2 * k),
        out_shape=[part] * (2 * k),
        compiler_params=pltpu.CompilerParams(vmem_limit_bytes=24 << 20),
        cost_estimate=pl.CostEstimate(
            flops=2 * k * n * (1 << 22), bytes_accessed=(3 << 20) + 2 * k * n * 32768, transcendentals=0
        ),
        name="weight_parts",
    )(rows, cols, up_slots, down_slots, x, dy, ht, dt)
    return outs[:k], outs[k:]


def token_kernel(rows, cols, meta, theirs, mine, h_ref, d_ref, up_ref, down_ref, send_ref, keep_ref, mix_acc, in_acc):
    step = pl.program_id(0)
    count = meta[0]

    @pl.when(step == 0)
    def _():
        mix_acc[...] = jnp.zeros_like(mix_acc)
        in_acc[...] = jnp.zeros_like(in_acc)

    for s in range(GROUP):
        slot = step * GROUP + s
        live = slot < count
        r = rows[slot]
        c = cols[slot]
        up = up_ref[0, s]
        down = down_ref[0, s]
        up = jnp.where(live, up, jnp.zeros_like(up))
        down = jnp.where(live, down, jnp.zeros_like(down))
        mix_acc[c] += nn(h_ref[r], down)
        in_acc[c] += nt(d_ref[r], up)

    @pl.when(step == STEPS - 1)
    def _():
        for k in range(8):
            for b in range(2):
                lanes = slice(b * SIDE, (b + 1) * SIDE)
                at = theirs[k] * 2 + b
                send_ref[k, 0, :, lanes] = mix_acc[at].astype(BF)
                send_ref[k, 1, :, lanes] = in_acc[at].astype(BF)
                at = mine[k] * 2 + b
                keep_ref[k, 0, :, lanes] = mix_acc[at].astype(BF)
                keep_ref[k, 1, :, lanes] = in_acc[at].astype(BF)


def token_parts(rows, cols, meta, theirs, mine, h, d, up_tiles, down_tiles):
    block = pl.BlockSpec((1, GROUP, SIDE, SIDE), lambda i: (0, i, 0, 0))
    part = jax.ShapeDtypeStruct((8, 2, SIDE, 2 * SIDE), BF)
    return pl.pallas_call(
        token_kernel,
        grid=(STEPS,),
        in_specs=[sspec()] * 5 + [vspec()] * 2 + [block] * 2,
        out_specs=[vspec()] * 2,
        out_shape=[part] * 2,
        scratch_shapes=[VM((COLS, SIDE, SIDE), F32)] * 2,
        compiler_params=pltpu.CompilerParams(vmem_limit_bytes=24 << 20),
        cost_estimate=pl.CostEstimate(flops=1 << 30, bytes_accessed=11 << 20, transcendentals=0),
        name="token_parts",
    )(rows, cols, meta, theirs, mine, h, d, up_tiles, down_tiles)


def pair_kernel(keep_ref, got_ref, *outs):
    for k in range(8):
        outs[k][...] = (keep_ref[k].astype(F32) + got_ref[k].astype(F32)).astype(BF)


def pair_sum(keep, got):
    part = jax.ShapeDtypeStruct((2, SIDE, 2 * SIDE), BF)
    return pl.pallas_call(
        pair_kernel,
        in_specs=[vspec()] * 2,
        out_specs=[vspec()] * 8,
        out_shape=[part] * 8,
        cost_estimate=pl.CostEstimate(flops=1 << 19, bytes_accessed=3 << 20, transcendentals=0),
        name="pair_sum",
    )(keep, got)


def ring(n, by):
    return [(i, (i + by) % n) for i in range(n)]


def step_both(x):
    pairs = []
    for z in range(8):
        pairs.append((z * 2, ((z + 1) % 8) * 2))
        pairs.append((z * 2 + 1, ((z - 1) % 8) * 2 + 1))
    return lax.ppermute(x, ("z", "c"), pairs)


def swap(x):
    return lax.ppermute(x, "c", [(0, 1), (1, 0)])


def add(*parts):
    total = parts[0].astype(F32)
    for p in parts[1:]:
        total = total + p.astype(F32)
    return total


def gather_over_tile(own, z, c):
    other = swap(own)
    first, second = own, other
    shards = [own, other]
    owners = [z * 2 + c, z * 2 + 1 - c]
    ahead = jnp.where(c == 0, -1, 1)
    for k in range(1, 5):
        first = step_both(first)
        behind = jnp.mod(z + k * ahead, 8) * 2
        beyond = jnp.mod(z - k * ahead, 8) * 2
        shards += [first, swap(first)]
        owners += [behind + c, beyond + 1 - c]
        if k < 4:
            second = step_both(second)
            shards += [second, swap(second)]
            owners += [behind + 1 - c, beyond + c]
    return shards, jnp.stack(owners).astype(jnp.int32)


def scatter_ring(axis, opp, right, left):
    up, down = ring(4, 1), ring(4, -1)
    from_left = lax.ppermute(opp[0], axis, up)
    from_right = lax.ppermute(opp[1], axis, down)
    left_b = lax.ppermute(right[1], axis, up)
    right_a = lax.ppermute(left[0], axis, down)
    left_a = lax.ppermute(add(right[0], from_left).astype(BF), axis, up)
    right_b = lax.ppermute(add(left[1], from_right).astype(BF), axis, down)
    return (left_a, right_a), (left_b, right_b)


def second_stage(axis, own, got):
    a = add(own[0], *got[0]).astype(BF)
    b = add(own[1], *got[1]).astype(BF)
    opp, right, left, mine = a[:8], a[8:], b[:8], b[8:]
    halves = scatter_ring(axis, (opp[:4], opp[4:]), (right[:4], right[4:]), (left[:4], left[4:]))
    return jnp.concatenate([add(mine[:4], *halves[0]), add(mine[4:], *halves[1])], axis=0)


def body(tokens, grad_out, up_tiles, down_tiles, tile_rows, tile_cols, tile_count):
    y, x = lax.axis_index("y"), lax.axis_index("x")
    z, c = lax.axis_index("z"), lax.axis_index("c")
    rows, cols = tile_rows[0], tile_cols[0]
    meta = tile_count.astype(jnp.int32)
    shards, owners = gather_over_tile(jnp.stack([tokens, grad_out]), z, c)
    x_all, dy_all, h, ht, d, dt = forward(rows, cols, meta, owners, shards, up_tiles, down_tiles)

    away = jnp.array([2, 1, -1, 0], jnp.int32)
    near = jnp.arange(8, dtype=jnp.int32)
    ys, xs = jnp.mod(y + away, 4), jnp.mod(x + away, 4)
    up_slots = ((ys[None, :, None] * 4 + xs[:, None, None]) * 8 + near).reshape(-1)
    down_slots = ((ys[:, None, None] * 4 + xs[None, :, None]) * 8 + near).reshape(-1)
    parts = functools.partial(weight_parts, rows, cols)
    up_opp, down_opp = parts(up_slots[:32], down_slots[:32], x_all, dy_all, ht, dt, 16)
    up_rest, down_rest = parts(up_slots[32:], down_slots[32:], x_all, dy_all, ht, dt, 16)
    up_got = scatter_ring("x", up_opp, up_rest[0:2], up_rest[2:4])
    down_got = scatter_ring("y", down_opp, down_rest[0:2], down_rest[2:4])

    k = jnp.arange(8, dtype=jnp.int32)
    to = jnp.mod(z + k, 8) * 2
    send, keep = token_parts(rows, cols, meta, to + 1 - c, to + c, h, d, up_tiles, down_tiles)
    pieces = pair_sum(keep, swap(send))
    terms = [pieces[0]] + [lax.ppermute(pieces[k], "z", ring(8, k)) for k in range(1, 8)]
    total = add(*terms).astype(BF)

    up_total = second_stage("y", up_rest[4:6], up_got)
    down_total = second_stage("x", down_rest[4:6], down_got)
    live = ((y * 4 + x) * 8 + near < meta[0])[:, None, None]
    grad_up = jnp.where(live, jnp.swapaxes(up_total, 1, 2) * (1.0 / 16), 0.0)
    grad_down = jnp.where(live, down_total * (1.0 / 16), 0.0)
    return total[0], total[1], grad_up[None], grad_down[None]


def solution(mesh):
    grid = Mesh(mesh.devices.reshape(4, 4, 8, 2), ("y", "x", "z", "c"))
    dp, tile = ("y", "x"), ("z", "c")
    placed = (
        P(dp, tile),
        P(dp, tile),
        P(tile, None, None, None),
        P(tile, None, None, None),
        P(tile, None),
        P(tile, None),
        P(tile),
    )
    return jax.shard_map(
        body,
        mesh=grid,
        in_specs=placed,
        out_specs=(P(dp, tile), P(dp, tile), P(tile, dp, None, None), P(tile, dp, None, None)),
        check_vma=False,
    )
```

```python
import functools

import jax
import jax.numpy as jnp
from jax import lax
from jax.experimental import pallas as pl
from jax.experimental.pallas import tpu as pltpu
from jax.sharding import Mesh, PartitionSpec as P

SIDE = 128
COLS = 32
ROWS = 8
SLOTS = 128
GROUP = 16
STEPS = SLOTS // GROUP
VM = pltpu.VMEM
SM = pltpu.SMEM
BF = jnp.bfloat16
F32 = jnp.float32


def whole(*shape):
    return pl.BlockSpec(shape, lambda *i: (0,) * len(shape))


def params(**kw):
    return pltpu.CompilerParams(vmem_limit_bytes=32 << 20, **kw)


def sspec():
    return pl.BlockSpec(memory_space=SM)


def nn(a, b):
    return jnp.dot(a, b, preferred_element_type=F32)


def nt(a, b):
    return lax.dot_general(a, b, (((1,), (1,)), ((), ())), preferred_element_type=F32)


def gelu_pair(pre):
    curve = lax.erf(pre * 0.7071067811865476)
    value = 0.5 * pre * (1.0 + curve)
    slope = 0.5 * (1.0 + curve) + pre * jnp.exp(-0.5 * pre * pre) * 0.3989422804014327
    return value, slope


def other_owner(k):
    z, c = lax.axis_index("z"), lax.axis_index("c")
    ahead = 2 * c - 1
    if k < 2:
        return z * 2 + (c if k == 0 else 1 - c)
    hop = (k - 2) // 4 + 1
    kind = (k - 2) % 4
    chip = z + hop * ahead if kind in (0, 2) else z - hop * ahead
    core = c if kind in (0, 3) else 1 - c
    return lax.rem(chip + 8, 8) * 2 + core


def forward_kernel(rows, cols, count_ref, *refs):
    shards = refs[:16]
    up_ref, down_ref = refs[16:18]
    x_ref, dy_ref, h_ref, ht_ref, d_ref, dt_ref = refs[18:24]
    pre_acc, gh_acc, sem = refs[24:27]
    step = pl.program_id(0)
    count = count_ref[0]

    @pl.when(step == 0)
    def _():
        copies = []
        for k in range(16):
            at = other_owner(k) * 2
            for b in range(2):
                lanes = pl.ds(b * SIDE, SIDE)
                copies.append(pltpu.make_async_copy(shards[k].at[0, :, lanes], x_ref.at[at + b], sem))
                copies.append(pltpu.make_async_copy(shards[k].at[1, :, lanes], dy_ref.at[at + b], sem))
        for copy in copies:
            copy.start()
        pre_acc[...] = jnp.zeros_like(pre_acc)
        gh_acc[...] = jnp.zeros_like(gh_acc)
        for copy in copies:
            copy.wait()

    for s in range(GROUP):
        slot = step * GROUP + s
        live = slot < count
        r = rows[slot]
        c = cols[slot]
        up = up_ref[0, s]
        down = down_ref[0, s]
        up = jnp.where(live, up, jnp.zeros_like(up))
        down = jnp.where(live, down, jnp.zeros_like(down))
        pre_acc[r] += nn(x_ref[c], up)
        gh_acc[r] += nt(dy_ref[c], down)

    @pl.when(step == STEPS - 1)
    def _():
        for r in range(ROWS):
            value, slope = gelu_pair(pre_acc[r])
            grad = gh_acc[r] * slope
            h_ref[r] = value.astype(BF)
            ht_ref[r] = value.T.astype(BF)
            d_ref[r] = grad.astype(BF)
            dt_ref[r] = grad.T.astype(BF)


def forward(rows, cols, count, shards, up_tiles, down_tiles):
    block = pl.BlockSpec((1, GROUP, SIDE, SIDE), lambda i: (0, i, 0, 0))
    tok = jax.ShapeDtypeStruct((COLS, SIDE, SIDE), BF)
    hid = jax.ShapeDtypeStruct((ROWS, SIDE, SIDE), BF)
    return pl.pallas_call(
        forward_kernel,
        grid=(STEPS,),
        in_specs=[sspec()] * 3 + [pl.BlockSpec(memory_space=pl.ANY)] * 16 + [block] * 2,
        out_specs=[whole(COLS, SIDE, SIDE)] * 2 + [whole(ROWS, SIDE, SIDE)] * 4,
        out_shape=[tok, tok, hid, hid, hid, hid],
        scratch_shapes=[VM((ROWS, SIDE, SIDE), F32)] * 2 + [pltpu.SemaphoreType.DMA],
        compiler_params=params(),
        cost_estimate=pl.CostEstimate(flops=1 << 30, bytes_accessed=12 << 20, transcendentals=1 << 18),
        name="forward",
    )(rows, cols, count, *shards, up_tiles, down_tiles)


def ring_slot(j):
    away = (2, 1, 3, 0)
    y = lax.rem(lax.axis_index("y") + away[j // 32], 4)
    x = lax.rem(lax.axis_index("x") + away[j // 8 % 4], 4)
    return (y * 4 + x) * 8 + j % 8


def weight_kernel(sizes, order, rows, cols, x_ref, t_ref, *outs):
    at = 0
    for out, n in zip(outs, sizes):
        for s in range(n):
            slot = order(at + s)
            out[s] = nn(t_ref[rows[slot]], x_ref[cols[slot]]).astype(BF)
        at += n


def weight_parts(rows, cols, x, t, sizes, order):
    return pl.pallas_call(
        functools.partial(weight_kernel, sizes, order),
        grid=(1,),
        in_specs=[sspec()] * 2 + [whole(COLS, SIDE, SIDE), whole(ROWS, SIDE, SIDE)],
        out_specs=[whole(n, SIDE, SIDE) for n in sizes],
        out_shape=[jax.ShapeDtypeStruct((n, SIDE, SIDE), BF) for n in sizes],
        compiler_params=params(),
        cost_estimate=pl.CostEstimate(flops=1 << 29, bytes_accessed=6 << 20, transcendentals=0),
        name="weight_parts",
    )(rows, cols, x, t)


def token_kernel(rows, cols, count_ref, h_ref, d_ref, up_ref, down_ref, send_ref, keep_ref, mix_acc, in_acc):
    step = pl.program_id(0)
    count = count_ref[0]

    @pl.when(step == 0)
    def _():
        mix_acc[...] = jnp.zeros_like(mix_acc)
        in_acc[...] = jnp.zeros_like(in_acc)

    for s in range(GROUP):
        slot = step * GROUP + s
        live = slot < count
        r = rows[slot]
        c = cols[slot]
        up = up_ref[0, s]
        down = down_ref[0, s]
        up = jnp.where(live, up, jnp.zeros_like(up))
        down = jnp.where(live, down, jnp.zeros_like(down))
        mix_acc[c] += nn(h_ref[r], down)
        in_acc[c] += nt(d_ref[r], up)

    @pl.when(step == STEPS - 1)
    def _():
        c = lax.axis_index("c")
        for k in range(8):
            for b in range(2):
                lanes = slice(b * SIDE, (b + 1) * SIDE)
                at = (2 * k + 1 - c) * 2 + b
                send_ref[k, 0, :, lanes] = mix_acc[at].astype(BF)
                send_ref[k, 1, :, lanes] = in_acc[at].astype(BF)
                at = (2 * k + c) * 2 + b
                keep_ref[k, 0, :, lanes] = mix_acc[at].astype(BF)
                keep_ref[k, 1, :, lanes] = in_acc[at].astype(BF)


def token_parts(rows, cols, count, h, d, up_tiles, down_tiles):
    block = pl.BlockSpec((1, GROUP, SIDE, SIDE), lambda i: (0, i, 0, 0))
    part = jax.ShapeDtypeStruct((8, 2, SIDE, 2 * SIDE), BF)
    return pl.pallas_call(
        token_kernel,
        grid=(STEPS,),
        in_specs=[sspec()] * 3 + [whole(ROWS, SIDE, SIDE)] * 2 + [block] * 2,
        out_specs=[whole(8, 2, SIDE, 2 * SIDE)] * 2,
        out_shape=[part] * 2,
        scratch_shapes=[VM((COLS, SIDE, SIDE), F32)] * 2,
        compiler_params=params(),
        cost_estimate=pl.CostEstimate(flops=1 << 30, bytes_accessed=11 << 20, transcendentals=0),
        name="token_parts",
    )(rows, cols, count, h, d, up_tiles, down_tiles)


def ring(n, by):
    return [(i, (i + by) % n) for i in range(n)]


def step_both(x):
    pairs = []
    for z in range(8):
        pairs.append((z * 2, ((z + 1) % 8) * 2))
        pairs.append((z * 2 + 1, ((z - 1) % 8) * 2 + 1))
    return lax.ppermute(x, ("z", "c"), pairs)


def swap(x):
    return lax.ppermute(x, "c", [(0, 1), (1, 0)])


def add(*parts):
    total = parts[0].astype(F32)
    for p in parts[1:]:
        total = total + p.astype(F32)
    return total


def gather_over_tile(own):
    first, second = own, swap(own)
    shards = [first, second]
    for k in range(1, 5):
        first = step_both(first)
        shards += [first, swap(first)]
        if k < 4:
            second = step_both(second)
            shards += [second, swap(second)]
    return shards


def scatter_ring(axis, opp_a, opp_b, right, left):
    n = opp_a.shape[0]
    up, down = ring(4, 1), ring(4, -1)
    from_left = lax.ppermute(opp_a, axis, up)
    from_right = lax.ppermute(opp_b, axis, down)
    right = lax.ppermute(right.at[:n].add(from_left), axis, up)
    left = lax.ppermute(left.at[n:].add(from_right), axis, down)
    return right, left


def body(tokens, grad_out, up_tiles, down_tiles, tile_rows, tile_cols, tile_count):
    rows, cols = tile_rows[0], tile_cols[0]
    shards = gather_over_tile(jnp.stack([tokens, grad_out]))
    x_all, dy_all, h, ht, d, dt = forward(rows, cols, tile_count, shards, up_tiles, down_tiles)
    opp_a, opp_b, right, left, mine = weight_parts(rows, cols, dy_all, ht, (16, 16, 32, 32, 32), ring_slot)
    (up_part,) = weight_parts(rows, cols, x_all, dt, (SLOTS,), lambda j: j)
    up_total = lax.psum_scatter(up_part, ("y", "x"), scatter_dimension=0, tiled=True)
    part = add(mine, *scatter_ring("y", opp_a, opp_b, right, left)).astype(BF)
    got = scatter_ring("x", part[:4], part[4:8], part[8:16], part[16:24])
    down_total = add(part[24:], *got)

    send, keep = token_parts(rows, cols, tile_count, h, d, up_tiles, down_tiles)
    pieces = add(keep, swap(send)).astype(BF)
    terms = lax.all_to_all(pieces, "z", 0, 0, tiled=True)
    total = jnp.sum(terms.astype(F32), axis=0).astype(BF)

    slot = lax.axis_index(("y", "x")) * 8 + jnp.arange(8, dtype=jnp.int32)
    live = (slot < tile_count[0])[:, None, None]
    grad_up = jnp.where(live, jnp.swapaxes(up_total, 1, 2).astype(F32) * (1.0 / 16), 0.0)
    grad_down = jnp.where(live, down_total * (1.0 / 16), 0.0)
    return total[0], total[1], grad_up[None], grad_down[None]


def solution(mesh):
    grid = Mesh(mesh.devices.reshape(4, 4, 8, 2), ("y", "x", "z", "c"))
    dp, tile = ("y", "x"), ("z", "c")
    placed = (
        P(dp, tile),
        P(dp, tile),
        P(tile, None, None, None),
        P(tile, None, None, None),
        P(tile, None),
        P(tile, None),
        P(tile),
    )
    return jax.shard_map(
        body,
        mesh=grid,
        in_specs=placed,
        out_specs=(P(dp, tile), P(dp, tile), P(tile, dp, None, None), P(tile, dp, None, None)),
        check_vma=False,
    )
```

```python
import functools

import jax
import jax.numpy as jnp
from jax import lax
from jax.experimental import pallas as pl
from jax.experimental.pallas import tpu as pltpu
from jax.sharding import Mesh, PartitionSpec as P

SIDE = 128
COLS = 32
ROWS = 8
SLOTS = 128
GROUP = 16
STEPS = SLOTS // GROUP
VM = pltpu.VMEM
SM = pltpu.SMEM
BF = jnp.bfloat16
F32 = jnp.float32


def whole(*shape):
    return pl.BlockSpec(shape, lambda *i: (0,) * len(shape))


def params(mib):
    return pltpu.CompilerParams(vmem_limit_bytes=mib << 20)


def sspec():
    return pl.BlockSpec(memory_space=SM)


def nn(a, b):
    return jnp.dot(a, b, preferred_element_type=F32)


def nt(a, b):
    return lax.dot_general(a, b, (((1,), (1,)), ((), ())), preferred_element_type=F32)


def gelu_pair(pre):
    curve = lax.erf(pre * 0.7071067811865476)
    value = 0.5 * pre * (1.0 + curve)
    slope = 0.5 * (1.0 + curve) + pre * jnp.exp(-0.5 * pre * pre) * 0.3989422804014327
    return value, slope


def other_owner(k):
    z, c = lax.axis_index("z"), lax.axis_index("c")
    ahead = 2 * c - 1
    if k < 2:
        return z * 2 + (c if k == 0 else 1 - c)
    hop = (k - 2) // 4 + 1
    kind = (k - 2) % 4
    chip = z + hop * ahead if kind in (0, 2) else z - hop * ahead
    core = c if kind in (0, 3) else 1 - c
    return lax.rem(chip + 8, 8) * 2 + core


def forward_kernel(rows, cols, count_ref, *refs):
    shards = refs[:16]
    up_ref, down_ref = refs[16:18]
    x_ref, dy_ref, h_ref, ht_ref, d_ref, dt_ref = refs[18:24]
    pre_acc, gh_acc, sem = refs[24:27]
    step = pl.program_id(0)
    count = count_ref[0]

    @pl.when(step == 0)
    def _():
        copies = []
        for k in range(16):
            at = other_owner(k) * 2
            for b in range(2):
                lanes = pl.ds(b * SIDE, SIDE)
                copies.append(pltpu.make_async_copy(shards[k].at[0, :, lanes], x_ref.at[at + b], sem))
                copies.append(pltpu.make_async_copy(shards[k].at[1, :, lanes], dy_ref.at[at + b], sem))
        for copy in copies:
            copy.start()
        pre_acc[...] = jnp.zeros_like(pre_acc)
        gh_acc[...] = jnp.zeros_like(gh_acc)
        for copy in copies:
            copy.wait()

    for s in range(GROUP):
        slot = step * GROUP + s
        live = slot < count
        r = rows[slot]
        c = cols[slot]
        up = up_ref[0, s]
        down = down_ref[0, s]
        up = jnp.where(live, up, jnp.zeros_like(up))
        down = jnp.where(live, down, jnp.zeros_like(down))
        pre_acc[r] += nn(x_ref[c], up)
        gh_acc[r] += nt(dy_ref[c], down)

    @pl.when(step == STEPS - 1)
    def _():
        for r in range(ROWS):
            value, slope = gelu_pair(pre_acc[r])
            grad = gh_acc[r] * slope
            h_ref[r] = value.astype(BF)
            ht_ref[r] = value.T.astype(BF)
            d_ref[r] = grad.astype(BF)
            dt_ref[r] = grad.T.astype(BF)


def forward(rows, cols, count, shards, up_tiles, down_tiles):
    block = pl.BlockSpec((1, GROUP, SIDE, SIDE), lambda i: (0, i, 0, 0))
    tok = jax.ShapeDtypeStruct((COLS, SIDE, SIDE), BF)
    hid = jax.ShapeDtypeStruct((ROWS, SIDE, SIDE), BF)
    return pl.pallas_call(
        forward_kernel,
        grid=(STEPS,),
        in_specs=[sspec()] * 3 + [pl.BlockSpec(memory_space=pl.ANY)] * 16 + [block] * 2,
        out_specs=[whole(COLS, SIDE, SIDE)] * 2 + [whole(ROWS, SIDE, SIDE)] * 4,
        out_shape=[tok, tok, hid, hid, hid, hid],
        scratch_shapes=[VM((ROWS, SIDE, SIDE), F32)] * 2 + [pltpu.SemaphoreType.DMA],
        compiler_params=params(48),
        cost_estimate=pl.CostEstimate(flops=1 << 30, bytes_accessed=12 << 20, transcendentals=1 << 18),
        name="forward",
    )(rows, cols, count, *shards, up_tiles, down_tiles)


def ring_slot(j, first, second):
    away = (2, 1, 3, 0)
    at = {
        first: lax.rem(lax.axis_index(first) + away[j // 32], 4),
        second: lax.rem(lax.axis_index(second) + away[j // 8 % 4], 4),
    }
    return (at["y"] * 4 + at["x"]) * 8 + j % 8


def weight_kernel(rows, cols, x_ref, dt_ref, dy_ref, ht_ref, *outs):
    up_outs, down_outs = outs[:7], outs[7:]

    def piece(axes, t_ref, v_ref, out, at):
        for s in range(out.shape[0]):
            slot = ring_slot(at + s, *axes)
            out[s] = nn(t_ref[rows[slot]], v_ref[cols[slot]]).astype(BF)

    for k in range(7):
        piece(("x", "y"), dt_ref, x_ref, up_outs[k], 16 * k)
        piece(("y", "x"), ht_ref, dy_ref, down_outs[k], 16 * k)


def weight_parts(rows, cols, x, dt, dy, ht):
    sizes = [16] * 6 + [32]
    outs = pl.pallas_call(
        weight_kernel,
        grid=(1,),
        in_specs=[sspec()] * 2 + [whole(COLS, SIDE, SIDE), whole(ROWS, SIDE, SIDE)] * 2,
        out_specs=[whole(n, SIDE, SIDE) for n in sizes * 2],
        out_shape=[jax.ShapeDtypeStruct((n, SIDE, SIDE), BF) for n in sizes * 2],
        compiler_params=params(32),
        cost_estimate=pl.CostEstimate(flops=1 << 30, bytes_accessed=12 << 20, transcendentals=0),
        name="weight_parts",
    )(rows, cols, x, dt, dy, ht)
    return outs[:7], outs[7:]


def token_kernel(rows, cols, count_ref, h_ref, d_ref, up_ref, down_ref, send_ref, keep_ref, mix_acc, in_acc):
    step = pl.program_id(0)
    count = count_ref[0]

    @pl.when(step == 0)
    def _():
        mix_acc[...] = jnp.zeros_like(mix_acc)
        in_acc[...] = jnp.zeros_like(in_acc)


    for s in range(GROUP):
        slot = step * GROUP + s
        live = slot < count
        r = rows[slot]
        c = cols[slot]
        up = up_ref[0, s]
        down = down_ref[0, s]
        up = jnp.where(live, up, jnp.zeros_like(up))
        down = jnp.where(live, down, jnp.zeros_like(down))
        mix_acc[c] += nn(h_ref[r], down)
        in_acc[c] += nt(d_ref[r], up)

    @pl.when(step == STEPS - 1)
    def _():
        c = lax.axis_index("c")
        for k in range(8):
            for b in range(2):
                lanes = slice(b * SIDE, (b + 1) * SIDE)
                at = (2 * k + 1 - c) * 2 + b
                send_ref[k, 0, :, lanes] = mix_acc[at].astype(BF)
                send_ref[k, 1, :, lanes] = in_acc[at].astype(BF)
                at = (2 * k + c) * 2 + b
                keep_ref[k, 0, :, lanes] = mix_acc[at].astype(BF)
                keep_ref[k, 1, :, lanes] = in_acc[at].astype(BF)


def token_parts(rows, cols, count, h, d, up_tiles, down_tiles):
    block = pl.BlockSpec((1, GROUP, SIDE, SIDE), lambda i: (0, i, 0, 0))
    part = jax.ShapeDtypeStruct((8, 2, SIDE, 2 * SIDE), BF)
    return pl.pallas_call(
        token_kernel,
        grid=(STEPS,),
        in_specs=[sspec()] * 3 + [whole(ROWS, SIDE, SIDE)] * 2 + [block] * 2,
        out_specs=[whole(8, 2, SIDE, 2 * SIDE)] * 2,
        out_shape=[part] * 2,
        scratch_shapes=[VM((COLS, SIDE, SIDE), F32)] * 2,
        compiler_params=params(48),
        cost_estimate=pl.CostEstimate(flops=1 << 30, bytes_accessed=11 << 20, transcendentals=0),
        name="token_parts",
    )(rows, cols, count, h, d, up_tiles, down_tiles)


def ring(n, by):
    return [(i, (i + by) % n) for i in range(n)]


def step_both(x):
    pairs = []
    for z in range(8):
        pairs.append((z * 2, ((z + 1) % 8) * 2))
        pairs.append((z * 2 + 1, ((z - 1) % 8) * 2 + 1))
    return lax.ppermute(x, ("z", "c"), pairs)


def swap(x):
    return lax.ppermute(x, "c", [(0, 1), (1, 0)])


def add(*parts):
    total = parts[0].astype(F32)
    for p in parts[1:]:
        total = total + p.astype(F32)
    return total


def gather_over_tile(own):
    first, second = own, swap(own)
    shards = [first, second]
    for k in range(1, 5):
        first = step_both(first)
        shards += [first, swap(first)]
        if k < 4:
            second = step_both(second)
            shards += [second, swap(second)]
    return shards


def hop(x, axis, by):
    return lax.ppermute(x, axis, ring(4, by))


def first_stage(axis, parts):
    far_a, far_b, next_a, next_b, before_a, before_b, own = parts
    from_left = hop(far_a, axis, 1)
    from_right = hop(far_b, axis, -1)
    left_b = hop(next_b, axis, 1)
    right_a = hop(before_a, axis, -1)
    left_a = hop(add(next_a, from_left).astype(BF), axis, 1)
    right_b = hop(add(before_b, from_right).astype(BF), axis, -1)
    return add(own[:16], left_a, right_a).astype(BF), add(own[16:], left_b, right_b).astype(BF)


def second_stage(axis, a, b):
    from_left = hop(a[:4], axis, 1)
    from_right = hop(a[4:8], axis, -1)
    left = hop(a[8:].at[:4].add(from_left), axis, 1)
    right = hop(b[:8].at[4:].add(from_right), axis, -1)
    return add(b[8:], left, right)


def body(tokens, grad_out, up_tiles, down_tiles, tile_rows, tile_cols, tile_count):
    rows, cols = tile_rows[0], tile_cols[0]
    shards = gather_over_tile(jnp.stack([tokens, grad_out]))
    x_all, dy_all, h, ht, d, dt = forward(rows, cols, tile_count, shards, up_tiles, down_tiles)
    up_parts, down_parts = weight_parts(rows, cols, x_all, dt, dy_all, ht)
    up_half = first_stage("x", up_parts)
    down_half = first_stage("y", down_parts)
    up_total = second_stage("y", *up_half)
    down_total = second_stage("x", *down_half)
    h, d, _, _ = lax.optimization_barrier((h, d, up_parts[0], down_parts[0]))

    send, keep = token_parts(rows, cols, tile_count, h, d, up_tiles, down_tiles)
    pieces = add(keep, swap(send)).astype(BF)
    terms = lax.all_to_all(pieces, "z", 0, 0, tiled=True)
    total = jnp.sum(terms.astype(F32), axis=0).astype(BF)

    slot = lax.axis_index(("y", "x")) * 8 + jnp.arange(8, dtype=jnp.int32)
    live = (slot < tile_count[0])[:, None, None]
    grad_up = jnp.where(live, jnp.swapaxes(up_total, 1, 2) * (1.0 / 16), 0.0)
    grad_down = jnp.where(live, down_total * (1.0 / 16), 0.0)
    return total[0], total[1], grad_up[None], grad_down[None]


def solution(mesh):
    grid = Mesh(mesh.devices.reshape(4, 4, 8, 2), ("y", "x", "z", "c"))
    dp, tile = ("y", "x"), ("z", "c")
    placed = (
        P(dp, tile),
        P(dp, tile),
        P(tile, None, None, None),
        P(tile, None, None, None),
        P(tile, None),
        P(tile, None),
        P(tile),
    )
    return jax.shard_map(
        body,
        mesh=grid,
        in_specs=placed,
        out_specs=(P(dp, tile), P(dp, tile), P(tile, dp, None, None), P(tile, dp, None, None)),
        check_vma=False,
    )
```

```python
import functools

import jax
import jax.numpy as jnp
from jax import lax
from jax.experimental import pallas as pl
from jax.experimental.pallas import tpu as pltpu
from jax.sharding import Mesh, PartitionSpec as P

SIDE = 128
COLS = 32
ROWS = 8
SLOTS = 128
GROUP = 16
STEPS = SLOTS // GROUP
VM = pltpu.VMEM
SM = pltpu.SMEM
BF = jnp.bfloat16
F32 = jnp.float32


def whole(*shape):
    return pl.BlockSpec(shape, lambda *i: (0,) * len(shape))


def params(mib):
    return pltpu.CompilerParams(vmem_limit_bytes=mib << 20)


def sspec():
    return pl.BlockSpec(memory_space=SM)


def nn(a, b):
    return jnp.dot(a, b, preferred_element_type=F32)


def nt(a, b):
    return lax.dot_general(a, b, (((1,), (1,)), ((), ())), preferred_element_type=F32)


def gelu_pair(pre):
    curve = lax.erf(pre * 0.7071067811865476)
    value = 0.5 * pre * (1.0 + curve)
    slope = 0.5 * (1.0 + curve) + pre * jnp.exp(-0.5 * pre * pre) * 0.3989422804014327
    return value, slope


def other_owner(k):
    z, c = lax.axis_index("z"), lax.axis_index("c")
    ahead = 2 * c - 1
    if k < 2:
        return z * 2 + (c if k == 0 else 1 - c)
    hop = (k - 2) // 4 + 1
    kind = (k - 2) % 4
    chip = z + hop * ahead if kind in (0, 2) else z - hop * ahead
    core = c if kind in (0, 3) else 1 - c
    return lax.rem(chip + 8, 8) * 2 + core


def forward_kernel(rows, cols, count_ref, *refs):
    shards = refs[:16]
    up_ref, down_ref = refs[16:18]
    x_ref, dy_ref, h_ref, ht_ref, d_ref, dt_ref = refs[18:24]
    pre_acc, gh_acc, sem = refs[24:27]
    step = pl.program_id(0)
    count = count_ref[0]

    @pl.when(step == 0)
    def _():
        copies = []
        for k in range(16):
            at = other_owner(k) * 2
            for b in range(2):
                lanes = pl.ds(b * SIDE, SIDE)
                copies.append(pltpu.make_async_copy(shards[k].at[0, :, lanes], x_ref.at[at + b], sem))
                copies.append(pltpu.make_async_copy(shards[k].at[1, :, lanes], dy_ref.at[at + b], sem))
        for copy in copies:
            copy.start()
        pre_acc[...] = jnp.zeros_like(pre_acc)
        gh_acc[...] = jnp.zeros_like(gh_acc)
        for copy in copies:
            copy.wait()

    for s in range(GROUP):
        slot = step * GROUP + s
        live = slot < count
        r = rows[slot]
        c = cols[slot]
        up = up_ref[0, s]
        down = down_ref[0, s]
        up = jnp.where(live, up, jnp.zeros_like(up))
        down = jnp.where(live, down, jnp.zeros_like(down))
        pre_acc[r] += nn(x_ref[c], up)
        gh_acc[r] += nt(dy_ref[c], down)

    @pl.when(step == STEPS - 1)
    def _():
        for r in range(ROWS):
            value, slope = gelu_pair(pre_acc[r])
            grad = gh_acc[r] * slope
            h_ref[r] = value.astype(BF)
            ht_ref[r] = value.T.astype(BF)
            d_ref[r] = grad.astype(BF)
            dt_ref[r] = grad.T.astype(BF)


def forward(rows, cols, count, shards, up_tiles, down_tiles):
    block = pl.BlockSpec((1, GROUP, SIDE, SIDE), lambda i: (0, i, 0, 0))
    tok = jax.ShapeDtypeStruct((COLS, SIDE, SIDE), BF)
    hid = jax.ShapeDtypeStruct((ROWS, SIDE, SIDE), BF)
    return pl.pallas_call(
        forward_kernel,
        grid=(STEPS,),
        in_specs=[sspec()] * 3 + [pl.BlockSpec(memory_space=pl.ANY)] * 16 + [block] * 2,
        out_specs=[whole(COLS, SIDE, SIDE)] * 2 + [whole(ROWS, SIDE, SIDE)] * 4,
        out_shape=[tok, tok, hid, hid, hid, hid],
        scratch_shapes=[VM((ROWS, SIDE, SIDE), F32)] * 2 + [pltpu.SemaphoreType.DMA],
        compiler_params=params(48),
        cost_estimate=pl.CostEstimate(flops=1 << 30, bytes_accessed=12 << 20, transcendentals=1 << 18),
        name="forward",
    )(rows, cols, count, *shards, up_tiles, down_tiles)


def ring_slot(j):
    first = ((2, 0), (2, 16), (1, 16), (3, 0), (1, 0), (3, 16), (0, 0), (0, 16))
    second = ((2, 0), (1, 4), (2, 4), (3, 0), (1, 0), (3, 4), (0, 0), (0, 4))
    away1, base = first[j // 16]
    place = base + j % 16
    away2, near = second[place // 4]
    c = lax.axis_index("c")
    away_x = away1 + c * (away2 - away1)
    away_y = away2 + c * (away1 - away2)
    y = lax.rem(lax.axis_index("y") + away_y, 4)
    x = lax.rem(lax.axis_index("x") + away_x, 4)
    return (y * 4 + x) * 8 + near + place % 4


SIZES = (16, 16, 16, 16, 16, 16, 32)


def weight_kernel(rows, cols, x_ref, dt_ref, dy_ref, ht_ref, *outs):
    at = 0
    for out, n in zip(outs, SIZES):
        for s in range(n):
            slot = ring_slot(at + s)
            row, col = rows[slot], cols[slot]
            out[0, s] = nn(dt_ref[row], x_ref[col]).astype(BF)
            out[1, s] = nn(ht_ref[row], dy_ref[col]).astype(BF)
        at += n


def weight_parts(rows, cols, x, dt, dy, ht):
    return pl.pallas_call(
        weight_kernel,
        grid=(1,),
        in_specs=[sspec()] * 2 + [whole(COLS, SIDE, SIDE), whole(ROWS, SIDE, SIDE)] * 2,
        out_specs=[whole(2, n, SIDE, SIDE) for n in SIZES],
        out_shape=[jax.ShapeDtypeStruct((2, n, SIDE, SIDE), BF) for n in SIZES],
        compiler_params=params(32),
        cost_estimate=pl.CostEstimate(flops=1 << 30, bytes_accessed=12 << 20, transcendentals=0),
        name="weight_parts",
    )(rows, cols, x, dt, dy, ht)


def token_kernel(rows, cols, count_ref, h_ref, d_ref, up_ref, down_ref, send_ref, keep_ref, mix_acc, in_acc):
    step = pl.program_id(0)
    count = count_ref[0]

    @pl.when(step == 0)
    def _():
        mix_acc[...] = jnp.zeros_like(mix_acc)
        in_acc[...] = jnp.zeros_like(in_acc)


    for s in range(GROUP):
        slot = step * GROUP + s
        live = slot < count
        r = rows[slot]
        c = cols[slot]
        up = up_ref[0, s]
        down = down_ref[0, s]
        up = jnp.where(live, up, jnp.zeros_like(up))
        down = jnp.where(live, down, jnp.zeros_like(down))
        mix_acc[c] += nn(h_ref[r], down)
        in_acc[c] += nt(d_ref[r], up)

    @pl.when(step == STEPS - 1)
    def _():
        c = lax.axis_index("c")
        for k in range(8):
            for b in range(2):
                lanes = slice(b * SIDE, (b + 1) * SIDE)
                at = (2 * k + 1 - c) * 2 + b
                send_ref[k, 0, :, lanes] = mix_acc[at].astype(BF)
                send_ref[k, 1, :, lanes] = in_acc[at].astype(BF)
                at = (2 * k + c) * 2 + b
                keep_ref[k, 0, :, lanes] = mix_acc[at].astype(BF)
                keep_ref[k, 1, :, lanes] = in_acc[at].astype(BF)


def token_parts(rows, cols, count, h, d, up_tiles, down_tiles):
    block = pl.BlockSpec((1, GROUP, SIDE, SIDE), lambda i: (0, i, 0, 0))
    part = jax.ShapeDtypeStruct((8, 2, SIDE, 2 * SIDE), BF)
    return pl.pallas_call(
        token_kernel,
        grid=(STEPS,),
        in_specs=[sspec()] * 3 + [whole(ROWS, SIDE, SIDE)] * 2 + [block] * 2,
        out_specs=[whole(8, 2, SIDE, 2 * SIDE)] * 2,
        out_shape=[part] * 2,
        scratch_shapes=[VM((COLS, SIDE, SIDE), F32)] * 2,
        compiler_params=params(48),
        cost_estimate=pl.CostEstimate(flops=1 << 30, bytes_accessed=11 << 20, transcendentals=0),
        name="token_parts",
    )(rows, cols, count, h, d, up_tiles, down_tiles)


def ring(n, by):
    return [(i, (i + by) % n) for i in range(n)]


def step_both(x):
    pairs = []
    for z in range(8):
        pairs.append((z * 2, ((z + 1) % 8) * 2))
        pairs.append((z * 2 + 1, ((z - 1) % 8) * 2 + 1))
    return lax.ppermute(x, ("z", "c"), pairs)


def swap(x):
    return lax.ppermute(x, "c", [(0, 1), (1, 0)])


def add(*parts):
    total = parts[0].astype(F32)
    for p in parts[1:]:
        total = total + p.astype(F32)
    return total


def gather_over_tile(own):
    first, second = own, swap(own)
    shards = [first, second]
    for k in range(1, 5):
        first = step_both(first)
        shards += [first, swap(first)]
        if k < 4:
            second = step_both(second)
            shards += [second, swap(second)]
    return shards


def hop(t, stage, by):
    pairs = []
    for y in range(4):
        for x in range(4):
            for c in range(2):
                along_x = (stage + c) % 2 == 0
                to_y = y if along_x else (y + by) % 4
                to_x = (x + by) % 4 if along_x else x
                pairs.append(((y * 4 + x) * 2 + c, (to_y * 4 + to_x) * 2 + c))
    return lax.ppermute(t, ("y", "x", "c"), pairs)


def send_far(parts):
    far_a, far_b, next_b, before_a = parts[:4]
    return hop(far_a, 0, 1), hop(far_b, 0, -1), hop(next_b, 0, 1), hop(before_a, 0, -1)


def two_stages(far, next_a, before_b, own):
    from_left, from_right, left_b, right_a = far
    left_a = hop(add(next_a, from_left).astype(BF), 0, 1)
    right_b = hop(add(before_b, from_right).astype(BF), 0, -1)

    def total(k, n):
        left, right = (left_a, right_a) if k < 16 else (left_b, right_b)
        at = slice(k % 16, k % 16 + n)
        return add(own[:, k : k + n], left[:, at], right[:, at])

    from_left = hop(total(0, 8).astype(BF), 1, 1)
    from_right = hop(total(8, 8).astype(BF), 1, -1)
    end_a = hop(add(total(16, 4), from_left[:, :4]).astype(BF), 1, 1)
    end_b = hop(add(total(20, 4), from_right[:, :4]).astype(BF), 1, -1)
    half_a = add(total(24, 4), end_a, from_right[:, 4:])
    half_b = add(total(28, 4), from_left[:, 4:], end_b)
    return jnp.concatenate([half_a, half_b], axis=1)


def body(tokens, grad_out, up_tiles, down_tiles, tile_rows, tile_cols, tile_count):
    rows, cols = tile_rows[0], tile_cols[0]
    shards = gather_over_tile(jnp.stack([tokens, grad_out]))
    x_all, dy_all, h, ht, d, dt = forward(rows, cols, tile_count, shards, up_tiles, down_tiles)
    parts = weight_parts(rows, cols, x_all, dt, dy_all, ht)
    far = send_far(parts)
    h, d, _ = lax.optimization_barrier((h, d, parts[0]))
    send, keep = token_parts(rows, cols, tile_count, h, d, up_tiles, down_tiles)
    pieces = add(keep, swap(send)).astype(BF)
    pieces, next_a, before_b = lax.optimization_barrier((pieces, parts[4], parts[5]))
    weights = two_stages(far, next_a, before_b, parts[6]) * (1.0 / 16)
    terms = lax.all_to_all(pieces, "z", 0, 0, tiled=True)
    total = jnp.sum(terms.astype(F32), axis=0).astype(BF)

    slot = lax.axis_index(("y", "x")) * 8 + jnp.arange(8, dtype=jnp.int32)
    live = (slot < tile_count[0])[:, None, None]
    grad_up = jnp.where(live, jnp.swapaxes(weights[0], 1, 2), 0.0)
    grad_down = jnp.where(live, weights[1], 0.0)
    return total[0], total[1], grad_up[None], grad_down[None]


def solution(mesh):
    grid = Mesh(mesh.devices.reshape(4, 4, 8, 2), ("y", "x", "z", "c"))
    dp, tile = ("y", "x"), ("z", "c")
    placed = (
        P(dp, tile),
        P(dp, tile),
        P(tile, None, None, None),
        P(tile, None, None, None),
        P(tile, None),
        P(tile, None),
        P(tile),
    )
    return jax.shard_map(
        body,
        mesh=grid,
        in_specs=placed,
        out_specs=(P(dp, tile), P(dp, tile), P(tile, dp, None, None), P(tile, dp, None, None)),
        check_vma=False,
    )
```

```python
import functools

import jax
import jax.numpy as jnp
from jax import lax
from jax.experimental import pallas as pl
from jax.experimental.pallas import tpu as pltpu
from jax.sharding import Mesh, PartitionSpec as P

SIDE = 128
COLS = 32
ROWS = 8
DENSE_MIB, FORWARD_MIB, TOKEN_MIB = 16, 16, 16
VM = pltpu.VMEM
SM = pltpu.SMEM
BF = jnp.bfloat16
F32 = jnp.float32


def whole(*shape):
    return pl.BlockSpec(shape, lambda *i: (0,) * len(shape))


def params(mib):
    return pltpu.CompilerParams(vmem_limit_bytes=mib << 20)


def sspec():
    return pl.BlockSpec(memory_space=SM)


def nn(a, b):
    return jnp.dot(a, b, preferred_element_type=F32)


def nt(a, b):
    return lax.dot_general(a, b, (((1,), (1,)), ((), ())), preferred_element_type=F32)


def gelu_pair(pre):
    curve = lax.erf(pre * 0.7071067811865476)
    value = 0.5 * pre * (1.0 + curve)
    slope = 0.5 * (1.0 + curve) + pre * jnp.exp(-0.5 * pre * pre) * 0.3989422804014327
    return value, slope


def other_owner(k):
    z, c = lax.axis_index("z"), lax.axis_index("c")
    ahead = 2 * c - 1
    if k < 2:
        return z * 2 + (c if k == 0 else 1 - c)
    hop = (k - 2) // 4 + 1
    kind = (k - 2) % 4
    chip = z + hop * ahead if kind in (0, 2) else z - hop * ahead
    core = c if kind in (0, 3) else 1 - c
    return lax.rem(chip + 8, 8) * 2 + core


def dense_kernel(rows, cols, count_ref, up_ref, down_ref, wu_ref, wd_ref, sem):
    count = count_ref[0]
    wu_ref[...] = jnp.zeros_like(wu_ref)
    wd_ref[...] = jnp.zeros_like(wd_ref)

    def copies(s):
        row = pl.ds(pl.multiple_of(rows[s] * SIDE, SIDE), SIDE)
        col = pl.ds(pl.multiple_of(cols[s] * SIDE, SIDE), SIDE)
        return (
            pltpu.make_async_copy(up_ref.at[0, s], wu_ref.at[col, row], sem),
            pltpu.make_async_copy(down_ref.at[0, s], wd_ref.at[row, col], sem),
        )

    @pl.loop(0, count)
    def _(s):
        for copy in copies(s):
            copy.start()

    @pl.loop(0, count)
    def _(s):
        for copy in copies(s):
            copy.wait()


def dense(rows, cols, count, up_tiles, down_tiles):
    return pl.pallas_call(
        dense_kernel,
        in_specs=[sspec()] * 3 + [pl.BlockSpec(memory_space=pltpu.HBM)] * 2,
        out_specs=[pl.BlockSpec(memory_space=VM)] * 2,
        out_shape=[
            jax.ShapeDtypeStruct((COLS * SIDE, ROWS * SIDE), BF),
            jax.ShapeDtypeStruct((ROWS * SIDE, COLS * SIDE), BF),
        ],
        scratch_shapes=[pltpu.SemaphoreType.DMA],
        compiler_params=params(DENSE_MIB),
        cost_estimate=pl.CostEstimate(flops=0, bytes_accessed=24 << 20, transcendentals=0),
        name="dense",
    )(rows, cols, count, up_tiles, down_tiles)


def lanes(k, n):
    return pl.ds(pl.multiple_of(k * n, n), n)


def forward_kernel(rows, cols, *refs):
    shards = refs[:16]
    wu_ref, wd_ref, h_ref, d_ref = refs[16:20]
    parts = refs[20:27]
    x_ref, dy_ref, ht_ref, dt_ref, sem = refs[27:32]
    wide = 2 * SIDE
    copies = []
    for k in range(16):
        at = lanes(other_owner(k), wide)
        copies.append(pltpu.make_async_copy(shards[k].at[0], x_ref.at[:, at], sem))
        copies.append(pltpu.make_async_copy(shards[k].at[1], dy_ref.at[:, at], sem))
    for copy in copies:
        copy.start()
    for copy in copies:
        copy.wait()
    for n in range(ROWS // 2):
        at = slice(n * wide, (n + 1) * wide)
        pre = nn(x_ref[...], wu_ref[:, at])
        grad_hidden = nt(dy_ref[...], wd_ref[at, :])
        value, slope = gelu_pair(pre)
        grad = grad_hidden * slope
        h_ref[:, at] = value.astype(BF)
        d_ref[:, at] = grad.astype(BF)
        for b in range(2):
            half = slice(b * SIDE, (b + 1) * SIDE)
            ht_ref[2 * n + b] = value[:, half].T.astype(BF)
            dt_ref[2 * n + b] = grad[:, half].T.astype(BF)
    at = 0
    for out, n in zip(parts, SIZES):
        for s in range(n):
            slot = ring_slot(at + s)
            row, col = rows[slot], lanes(cols[slot], SIDE)
            out[0, s] = nn(dt_ref[row], x_ref[:, col]).astype(BF)
            out[1, s] = nn(ht_ref[row], dy_ref[:, col]).astype(BF)
        at += n


def forward(rows, cols, shards, wu, wd):
    hid = jax.ShapeDtypeStruct((SIDE, ROWS * SIDE), BF)
    anywhere = pl.BlockSpec(memory_space=pl.ANY)
    return pl.pallas_call(
        forward_kernel,
        in_specs=[sspec()] * 2 + [anywhere] * 16 + [pl.BlockSpec(memory_space=VM)] * 2,
        out_specs=[pl.BlockSpec(memory_space=VM)] * 9,
        out_shape=[hid, hid] + [jax.ShapeDtypeStruct((2, n, SIDE, SIDE), BF) for n in SIZES],
        scratch_shapes=[VM((SIDE, COLS * SIDE), BF)] * 2
        + [VM((ROWS, SIDE, SIDE), BF)] * 2
        + [pltpu.SemaphoreType.DMA],
        compiler_params=params(FORWARD_MIB),
        cost_estimate=pl.CostEstimate(flops=3 << 30, bytes_accessed=28 << 20, transcendentals=1 << 18),
        name="forward",
    )(rows, cols, *shards, wu, wd)


def ring_slot(j):
    first = ((2, 0), (2, 16), (1, 16), (3, 0), (1, 0), (3, 16), (0, 0), (0, 16))
    second = ((2, 0), (1, 4), (2, 4), (3, 0), (1, 0), (3, 4), (0, 0), (0, 4))
    away1, base = first[j // 16]
    place = base + j % 16
    away2, near = second[place // 4]
    c = lax.axis_index("c")
    away_x = away1 + c * (away2 - away1)
    away_y = away2 + c * (away1 - away2)
    y = lax.rem(lax.axis_index("y") + away_y, 4)
    x = lax.rem(lax.axis_index("x") + away_x, 4)
    return (y * 4 + x) * 8 + near + place % 4


SIZES = (16, 16, 16, 16, 16, 16, 32)


def token_kernel(h_ref, d_ref, wu_ref, wd_ref, send_ref, keep_ref):
    wide = 2 * SIDE
    c = lax.axis_index("c")
    for out, core in ((send_ref, 1 - c), (keep_ref, c)):
        for k in range(8):
            at = lanes(2 * k + core, wide)
            out[k, 0] = nn(h_ref[...], wd_ref[:, at]).astype(BF)
            out[k, 1] = nt(d_ref[...], wu_ref[at, :]).astype(BF)


def token_parts(h, d, wu, wd):
    part = jax.ShapeDtypeStruct((8, 2, SIDE, 2 * SIDE), BF)
    return pl.pallas_call(
        token_kernel,
        in_specs=[pl.BlockSpec(memory_space=VM)] * 4,
        out_specs=[pl.BlockSpec(memory_space=VM)] * 2,
        out_shape=[part] * 2,
        compiler_params=params(TOKEN_MIB),
        cost_estimate=pl.CostEstimate(flops=2 << 30, bytes_accessed=19 << 20, transcendentals=0),
        name="token_parts",
    )(h, d, wu, wd)


def ring(n, by):
    return [(i, (i + by) % n) for i in range(n)]


def step_both(x):
    pairs = []
    for z in range(8):
        pairs.append((z * 2, ((z + 1) % 8) * 2))
        pairs.append((z * 2 + 1, ((z - 1) % 8) * 2 + 1))
    return lax.ppermute(x, ("z", "c"), pairs)


def swap(x):
    return lax.ppermute(x, "c", [(0, 1), (1, 0)])


def add(*parts):
    total = parts[0].astype(F32)
    for p in parts[1:]:
        total = total + p.astype(F32)
    return total


def gather_over_tile(own, wu, wd):
    first, second = own, swap(own)
    shards = [first, second]
    for k in range(1, 5):
        if k == 3:
            first, wu, wd = lax.optimization_barrier((first, wu, wd))
        first = step_both(first)
        shards += [first, swap(first)]
        if k < 4:
            second = step_both(second)
            shards += [second, swap(second)]
    return shards, wu, wd


def hop(t, stage, by):
    pairs = []
    for y in range(4):
        for x in range(4):
            for c in range(2):
                along_x = (stage + c) % 2 == 0
                to_y = y if along_x else (y + by) % 4
                to_x = (x + by) % 4 if along_x else x
                pairs.append(((y * 4 + x) * 2 + c, (to_y * 4 + to_x) * 2 + c))
    return lax.ppermute(t, ("y", "x", "c"), pairs)


def send_far(parts):
    far_a, far_b, next_b, before_a = parts[:4]
    return hop(far_a, 0, 1), hop(far_b, 0, -1), hop(next_b, 0, 1), hop(before_a, 0, -1)


def two_stages(far, next_a, before_b, own, pieces):
    from_left, from_right, left_b, right_a = far
    left_a = hop(add(next_a, from_left).astype(BF), 0, 1)
    right_b = hop(add(before_b, from_right).astype(BF), 0, -1)

    def total(k, n):
        left, right = (left_a, right_a) if k < 16 else (left_b, right_b)
        at = slice(k % 16, k % 16 + n)
        return add(own[:, k : k + n], left[:, at], right[:, at])

    start = total(0, 8).astype(BF)
    start, pieces = lax.optimization_barrier((start, pieces))
    from_left = hop(start, 1, 1)
    from_right = hop(total(8, 8).astype(BF), 1, -1)
    end_a = hop(add(total(16, 4), from_left[:, :4]).astype(BF), 1, 1)
    end_b = hop(add(total(20, 4), from_right[:, :4]).astype(BF), 1, -1)
    half_a = add(total(24, 4), end_a, from_right[:, 4:])
    half_b = add(total(28, 4), from_left[:, 4:], end_b)
    return jnp.concatenate([half_a, half_b], axis=1), pieces


def body(tokens, grad_out, up_tiles, down_tiles, tile_rows, tile_cols, tile_count):
    rows, cols = tile_rows[0], tile_cols[0]
    wu, wd = dense(rows, cols, tile_count, up_tiles, down_tiles)
    shards, wu, wd = gather_over_tile(jnp.stack([tokens, grad_out]), wu, wd)
    h, d, *parts = forward(rows, cols, shards, wu, wd)
    far = send_far(parts)
    h, d, _ = lax.optimization_barrier((h, d, parts[0]))
    send, keep = token_parts(h, d, wu, wd)
    pieces = add(keep, swap(send)).astype(BF)
    weights, pieces = two_stages(far, parts[4], parts[5], parts[6], pieces)
    weights = weights * (1.0 / 16)
    terms = lax.all_to_all(pieces, "z", 0, 0, tiled=True)
    total = jnp.sum(terms.astype(F32), axis=0).astype(BF)

    slot = lax.axis_index(("y", "x")) * 8 + jnp.arange(8, dtype=jnp.int32)
    live = (slot < tile_count[0])[:, None, None]
    grad_up = jnp.where(live, jnp.swapaxes(weights[0], 1, 2), 0.0)
    grad_down = jnp.where(live, weights[1], 0.0)
    return total[0], total[1], grad_up[None], grad_down[None]


def solution(mesh):
    grid = Mesh(mesh.devices.reshape(4, 4, 8, 2), ("y", "x", "z", "c"))
    dp, tile = ("y", "x"), ("z", "c")
    placed = (
        P(dp, tile),
        P(dp, tile),
        P(tile, None, None, None),
        P(tile, None, None, None),
        P(tile, None),
        P(tile, None),
        P(tile),
    )
    return jax.shard_map(
        body,
        mesh=grid,
        in_specs=placed,
        out_specs=(P(dp, tile), P(dp, tile), P(tile, dp, None, None), P(tile, dp, None, None)),
        check_vma=False,
    )
```

```python
import functools

import jax
import jax.numpy as jnp
from jax import lax
from jax.experimental import pallas as pl
from jax.experimental.pallas import tpu as pltpu
from jax.sharding import Mesh, PartitionSpec as P

SIDE = 128
COLS = 32
ROWS = 8
VM = pltpu.VMEM
SM = pltpu.SMEM
BF = jnp.bfloat16
F32 = jnp.float32


def whole(*shape):
    return pl.BlockSpec(shape, lambda *i: (0,) * len(shape))


def vspec():
    return pl.BlockSpec(memory_space=VM)


def params(mib):
    return pltpu.CompilerParams(vmem_limit_bytes=mib << 20)


def sspec():
    return pl.BlockSpec(memory_space=SM)


def nn(a, b):
    return jnp.dot(a, b, preferred_element_type=F32)


def nt(a, b):
    return lax.dot_general(a, b, (((1,), (1,)), ((), ())), preferred_element_type=F32)


def gelu_pair(pre):
    curve = lax.erf(pre * 0.7071067811865476)
    value = 0.5 * pre * (1.0 + curve)
    slope = 0.5 * (1.0 + curve) + pre * jnp.exp(-0.5 * pre * pre) * 0.3989422804014327
    return value, slope


def other_owner(k):
    z, c = lax.axis_index("z"), lax.axis_index("c")
    ahead = 2 * c - 1
    if k < 2:
        return z * 2 + (c if k == 0 else 1 - c)
    hop = (k - 2) // 4 + 1
    kind = (k - 2) % 4
    chip = z + hop * ahead if kind in (0, 2) else z - hop * ahead
    core = c if kind in (0, 3) else 1 - c
    return lax.rem(chip + 8, 8) * 2 + core


def split(code):
    return code // COLS, lax.rem(code, COLS)


def dense_kernel(up, where, count_ref, tiles_ref, out_ref, sem):
    count = count_ref[0]
    out_ref[...] = jnp.zeros_like(out_ref)

    def copy(s):
        row, col = (lanes(k, SIDE) for k in split(where[s]))
        at = (col, row) if up else (row, col)
        return pltpu.make_async_copy(tiles_ref.at[0, s], out_ref.at[at], sem)

    @pl.loop(0, count)
    def _(s):
        copy(s).start()

    @pl.loop(0, count)
    def _(s):
        copy(s).wait()


def dense(where, count, tiles, up):
    features, hidden = COLS * SIDE, ROWS * SIDE
    return pl.pallas_call(
        functools.partial(dense_kernel, up),
        in_specs=[sspec()] * 2 + [pl.BlockSpec(memory_space=pltpu.HBM)],
        out_specs=vspec(),
        out_shape=jax.ShapeDtypeStruct((features, hidden) if up else (hidden, features), BF),
        scratch_shapes=[pltpu.SemaphoreType.DMA],
        compiler_params=params(16),
        cost_estimate=pl.CostEstimate(flops=0, bytes_accessed=12 << 20, transcendentals=0),
        name="dense_up" if up else "dense_down",
    )(where, count, tiles)


def lanes(k, n):
    return pl.ds(pl.multiple_of(k * n, n), n)


def forward_kernel(where, *refs):
    shards = refs[:16]
    wu_ref, wd_ref, h_ref, d_ref, x_ref, dy_ref, dt_ref, ht_ref = refs[16:24]
    parts, sem = refs[24:28], refs[28]
    wide = 2 * SIDE
    copies = []
    for k in range(16):
        at = lanes(other_owner(k), wide)
        copies.append(pltpu.make_async_copy(shards[k].at[0], x_ref.at[:, at], sem))
        copies.append(pltpu.make_async_copy(shards[k].at[1], dy_ref.at[:, at], sem))
    for copy in copies:
        copy.start()
    for copy in copies:
        copy.wait()
    for n in range(ROWS // 2):
        at = slice(n * wide, (n + 1) * wide)
        pre = nn(x_ref[...], wu_ref[:, at])
        grad_hidden = nt(dy_ref[...], wd_ref[at, :])
        value, slope = gelu_pair(pre)
        grad = grad_hidden * slope
        h_ref[:, at] = value.astype(BF)
        d_ref[:, at] = grad.astype(BF)
        for b in range(2):
            half = slice(b * SIDE, (b + 1) * SIDE)
            ht_ref[2 * n + b] = value[:, half].T.astype(BF)
            dt_ref[2 * n + b] = grad[:, half].T.astype(BF)
    fill_parts(where, x_ref, dy_ref, dt_ref, ht_ref, parts, ((2, 0, 2), (2, 2, 2)))


def fill_parts(where, x_ref, dy_ref, dt_ref, ht_ref, outs, blocks):
    for k, (away, start, n) in enumerate(blocks):

        @pl.loop(0, n)
        def _(group):
            first = ring_slot(away, start + group)
            for s in range(8):
                row, col = split(where[first + s])
                at = lanes(col, SIDE)
                outs[2 * k][group * 8 + s] = nn(dt_ref[row], x_ref[:, at]).astype(BF)
                outs[2 * k + 1][group * 8 + s] = nn(ht_ref[row], dy_ref[:, at]).astype(BF)


def forward(where, shards, wu, wd):
    hid = jax.ShapeDtypeStruct((SIDE, ROWS * SIDE), BF)
    tok = jax.ShapeDtypeStruct((SIDE, COLS * SIDE), BF)
    turned = jax.ShapeDtypeStruct((ROWS, SIDE, SIDE), BF)
    part = jax.ShapeDtypeStruct((16, SIDE, SIDE), BF)
    return pl.pallas_call(
        forward_kernel,
        in_specs=[sspec()] + [pl.BlockSpec(memory_space=pl.ANY)] * 16 + [vspec()] * 2,
        out_specs=[vspec()] * 10,
        out_shape=[hid, hid, tok, tok, turned, turned] + [part] * 4,
        scratch_shapes=[pltpu.SemaphoreType.DMA],
        compiler_params=params(16),
        cost_estimate=pl.CostEstimate(flops=3 << 30, bytes_accessed=22 << 20, transcendentals=1 << 18),
        name="forward",
    )(where, *shards, wu, wd)


def rest_kernel(where, x_ref, dy_ref, dt_ref, ht_ref, *outs):
    fill_parts(where, x_ref, dy_ref, dt_ref, ht_ref, outs, ((1, 0, 4), (3, 0, 4), (0, 0, 4)))


def rest_parts(where, x, dy, dt, ht):
    return pl.pallas_call(
        rest_kernel,
        in_specs=[sspec()] + [vspec()] * 4,
        out_specs=[vspec()] * 6,
        out_shape=[jax.ShapeDtypeStruct((32, SIDE, SIDE), BF)] * 6,
        compiler_params=params(16),
        cost_estimate=pl.CostEstimate(flops=1 << 30, bytes_accessed=9 << 20, transcendentals=0),
        name="rest_parts",
    )(where, x, dy, dt, ht)


def ring_slot(away1, group):
    away2 = jnp.where(group == 0, 2, jnp.where(group == 1, 1, jnp.where(group == 2, 3, 0)))
    c = lax.axis_index("c")
    away_x = away1 + c * (away2 - away1)
    away_y = away2 + c * (away1 - away2)
    y = lax.rem(lax.axis_index("y") + away_y, 4)
    x = lax.rem(lax.axis_index("x") + away_x, 4)
    return (y * 4 + x) * 8


def token_kernel(h_ref, d_ref, wu_ref, wd_ref, send_ref, keep_ref):
    wide = 2 * SIDE
    c = lax.axis_index("c")
    for out, core in ((send_ref, 1 - c), (keep_ref, c)):
        for k in range(8):
            at = lanes(2 * k + core, wide)
            out[k, 0] = nn(h_ref[...], wd_ref[:, at]).astype(BF)
            out[k, 1] = nt(d_ref[...], wu_ref[at, :]).astype(BF)


def token_parts(h, d, wu, wd):
    part = jax.ShapeDtypeStruct((8, 2, SIDE, 2 * SIDE), BF)
    return pl.pallas_call(
        token_kernel,
        in_specs=[vspec()] * 4,
        out_specs=[vspec()] * 2,
        out_shape=[part] * 2,
        compiler_params=params(16),
        cost_estimate=pl.CostEstimate(flops=2 << 30, bytes_accessed=19 << 20, transcendentals=0),
        name="token_parts",
    )(h, d, wu, wd)


def ring(n, by):
    return [(i, (i + by) % n) for i in range(n)]


def step_both(x):
    pairs = []
    for z in range(8):
        pairs.append((z * 2, ((z + 1) % 8) * 2))
        pairs.append((z * 2 + 1, ((z - 1) % 8) * 2 + 1))
    return lax.ppermute(x, ("z", "c"), pairs)


def swap(x):
    return lax.ppermute(x, "c", [(0, 1), (1, 0)])


def add(*parts):
    total = parts[0].astype(F32)
    for p in parts[1:]:
        total = total + p.astype(F32)
    return total


def gather_over_tile(own, wu, wd):
    first, second = own, swap(own)
    shards = [first, second]
    for k in range(1, 5):
        if k == 3:
            first, wu = lax.optimization_barrier((first, wu))
        if k == 4:
            first, wd = lax.optimization_barrier((first, wd))
        first = step_both(first)
        shards += [first, swap(first)]
        if k < 4:
            second = step_both(second)
            shards += [second, swap(second)]
    return shards, wu, wd


def hop(t, stage, by):
    pairs = []
    for y in range(4):
        for x in range(4):
            for c in range(2):
                along_x = (stage + c) % 2 == 0
                to_y = y if along_x else (y + by) % 4
                to_x = (x + by) % 4 if along_x else x
                pairs.append(((y * 4 + x) * 2 + c, (to_y * 4 + to_x) * 2 + c))
    return lax.ppermute(t, ("y", "x", "c"), pairs)


def send_two_ways(far_a, far_b, nearer, before, stage):
    n = far_a.shape[0]
    from_left = hop(far_a, stage, 1)
    from_right = hop(far_b, stage, -1)
    left = hop(nearer.at[:n].add(from_left), stage, 1)
    right = hop(before.at[n:].add(from_right), stage, -1)
    return left, right


def ring_sum(far_a, far_b, nearer, before, own):
    left, right = send_two_ways(far_a, far_b, nearer, before, 0)

    def total(k, n):
        return add(own[k : k + n], left[k : k + n], right[k : k + n])

    sent = (total(k, n).astype(BF) for k, n in ((0, 4), (4, 4), (8, 8), (16, 8)))
    return total(24, 8), *send_two_ways(*sent, 1)


def finish_kernel(count_ref, *refs):
    first = lax.axis_index(("y", "x")) * 8
    for k in range(2):
        base, left, right = refs[3 * k : 3 * k + 3]
        out = refs[6 + k]
        for s in range(8):
            total = base[s] + left[s].astype(F32) + right[s].astype(F32)
            total = jnp.where(first + s < count_ref[0], total * (1.0 / 16), 0.0)
            out[0, s] = total.T if k == 0 else total


def finish(count, up, down):
    shape = (1, 8, SIDE, SIDE)
    return pl.pallas_call(
        finish_kernel,
        grid=(1,),
        in_specs=[sspec()] + [whole(8, SIDE, SIDE)] * 6,
        out_specs=[whole(*shape)] * 2,
        out_shape=[jax.ShapeDtypeStruct(shape, F32)] * 2,
        compiler_params=params(16),
        cost_estimate=pl.CostEstimate(flops=1 << 20, bytes_accessed=3 << 20, transcendentals=0),
        name="finish",
    )(count, *up, *down)


def owner_sum_kernel(terms_ref, mixed_ref, grad_in_ref):
    for k, out in enumerate((mixed_ref, grad_in_ref)):
        total = terms_ref[0, k].astype(F32)
        for z in range(1, 8):
            total = total + terms_ref[z, k].astype(F32)
        out[...] = total.astype(BF)


def owner_sum(terms):
    shape = terms.shape[2:]
    return pl.pallas_call(
        owner_sum_kernel,
        grid=(1,),
        in_specs=[whole(*terms.shape)],
        out_specs=[whole(*shape)] * 2,
        out_shape=[jax.ShapeDtypeStruct(shape, BF)] * 2,
        compiler_params=params(16),
        cost_estimate=pl.CostEstimate(flops=1 << 19, bytes_accessed=1 << 20, transcendentals=0),
        name="owner_sum",
    )(terms)


def body(tokens, grad_out, up_tiles, down_tiles, tile_rows, tile_cols, tile_count):
    where = tile_rows[0] * COLS + tile_cols[0]
    wu = dense(where, tile_count, up_tiles, True)
    wd = dense(where, tile_count, down_tiles, False)
    shards, wu, wd = gather_over_tile(jnp.stack([tokens, grad_out]), wu, wd)
    h, d, x, dy, dt, ht, *far = forward(where, shards, wu, wd)
    rest = rest_parts(where, x, dy, dt, ht)
    h, d, _ = lax.optimization_barrier((h, d, rest[0]))
    send, keep = token_parts(h, d, wu, wd)
    pieces = add(keep, swap(send)).astype(BF)
    up = ring_sum(far[0], far[2], *rest[0::2])
    pieces, down_next = lax.optimization_barrier((pieces, rest[1]))
    down = ring_sum(far[1], far[3], down_next, rest[3], rest[5])
    mixed, grad_in = owner_sum(lax.all_to_all(pieces, "z", 0, 0, tiled=True))
    grad_up, grad_down = finish(tile_count, up, down)
    return mixed, grad_in, grad_up, grad_down


def solution(mesh):
    grid = Mesh(mesh.devices.reshape(4, 4, 8, 2), ("y", "x", "z", "c"))
    dp, tile = ("y", "x"), ("z", "c")
    placed = (
        P(dp, tile),
        P(dp, tile),
        P(tile, None, None, None),
        P(tile, None, None, None),
        P(tile, None),
        P(tile, None),
        P(tile),
    )
    return jax.shard_map(
        body,
        mesh=grid,
        in_specs=placed,
        out_specs=(P(dp, tile), P(dp, tile), P(tile, dp, None, None), P(tile, dp, None, None)),
        check_vma=False,
    )
```

```python
import functools

import jax
import jax.numpy as jnp
from jax import lax
from jax.experimental import pallas as pl
from jax.experimental.pallas import tpu as pltpu
from jax.sharding import Mesh, PartitionSpec as P

SIDE = 128
COLS = 32
ROWS = 8
VM = pltpu.VMEM
SM = pltpu.SMEM
BF = jnp.bfloat16
F32 = jnp.float32


def whole(*shape):
    return pl.BlockSpec(shape, lambda *i: (0,) * len(shape))


def vspec():
    return pl.BlockSpec(memory_space=VM)


def params(mib):
    return pltpu.CompilerParams(vmem_limit_bytes=mib << 20)


def sspec():
    return pl.BlockSpec(memory_space=SM)


def nn(a, b):
    return jnp.dot(a, b, preferred_element_type=F32)


def nt(a, b):
    return lax.dot_general(a, b, (((1,), (1,)), ((), ())), preferred_element_type=F32)


def gelu_pair(pre):
    curve = lax.erf(pre * 0.7071067811865476)
    value = 0.5 * pre * (1.0 + curve)
    slope = 0.5 * (1.0 + curve) + pre * jnp.exp(-0.5 * pre * pre) * 0.3989422804014327
    return value, slope


def other_owner(k):
    z, c = lax.axis_index("z"), lax.axis_index("c")
    ahead = 2 * c - 1
    if k < 2:
        return z * 2 + (c if k == 0 else 1 - c)
    hop = (k - 2) // 4 + 1
    kind = (k - 2) % 4
    chip = z + hop * ahead if kind in (0, 2) else z - hop * ahead
    core = c if kind in (0, 3) else 1 - c
    return lax.rem(chip + 8, 8) * 2 + core


def split(code):
    return code // COLS, lax.rem(code, COLS)


def dense_kernel(up, where, count_ref, tiles_ref, out_ref, sem):
    count = count_ref[0]
    out_ref[...] = jnp.zeros_like(out_ref)

    def copy(s):
        row, col = (lanes(k, SIDE) for k in split(where[s]))
        at = (col, row) if up else (row, col)
        return pltpu.make_async_copy(tiles_ref.at[0, s], out_ref.at[at], sem)

    @pl.loop(0, count)
    def _(s):
        copy(s).start()

    @pl.loop(0, count)
    def _(s):
        copy(s).wait()


def dense(where, count, tiles, up):
    features, hidden = COLS * SIDE, ROWS * SIDE
    return pl.pallas_call(
        functools.partial(dense_kernel, up),
        in_specs=[sspec()] * 2 + [pl.BlockSpec(memory_space=pltpu.HBM)],
        out_specs=vspec(),
        out_shape=jax.ShapeDtypeStruct((features, hidden) if up else (hidden, features), BF),
        scratch_shapes=[pltpu.SemaphoreType.DMA],
        compiler_params=params(16),
        cost_estimate=pl.CostEstimate(flops=0, bytes_accessed=12 << 20, transcendentals=0),
        name="dense_up" if up else "dense_down",
    )(where, count, tiles)


def lanes(k, n):
    return pl.ds(pl.multiple_of(k * n, n), n)


def forward_kernel(where, *refs):
    shards = refs[:16]
    wu_ref, wd_ref, h_ref, d_ref, x_ref, dy_ref, dt_ref, ht_ref = refs[16:24]
    parts, sem = refs[24:26], refs[26]
    wide = 2 * SIDE
    copies = []
    for k in range(16):
        at = lanes(other_owner(k), wide)
        copies.append(pltpu.make_async_copy(shards[k].at[0], x_ref.at[:, at], sem))
        copies.append(pltpu.make_async_copy(shards[k].at[1], dy_ref.at[:, at], sem))
    for copy in copies:
        copy.start()
    for copy in copies:
        copy.wait()

    @pl.loop(0, ROWS // 2)
    def _(n):
        at = lanes(n, wide)
        pre = nn(x_ref[...], wu_ref[:, at])
        grad_hidden = nt(dy_ref[...], wd_ref[at, :])
        value, slope = gelu_pair(pre)
        grad = grad_hidden * slope
        h_ref[:, at] = value.astype(BF)
        d_ref[:, at] = grad.astype(BF)
        for b in range(2):
            half = slice(b * SIDE, (b + 1) * SIDE)
            ht_ref[2 * n + b] = value[:, half].T.astype(BF)
            dt_ref[2 * n + b] = grad[:, half].T.astype(BF)

    fill_parts(where, x_ref, dy_ref, dt_ref, ht_ref, parts, ((2, 0, 16), (2, 16, 16)))


def fill_parts(where, x_ref, dy_ref, dt_ref, ht_ref, outs, blocks):
    for out, (away, start, n) in zip(outs, blocks):
        for s in range(n):
            row, col = split(where[ring_slot(away, start + s)])
            at = lanes(col, SIDE)
            out[0, s] = nn(dt_ref[row], x_ref[:, at]).astype(BF)
            out[1, s] = nn(ht_ref[row], dy_ref[:, at]).astype(BF)


def forward(where, shards, wu, wd):
    hid = jax.ShapeDtypeStruct((SIDE, ROWS * SIDE), BF)
    tok = jax.ShapeDtypeStruct((SIDE, COLS * SIDE), BF)
    turned = jax.ShapeDtypeStruct((ROWS, SIDE, SIDE), BF)
    part = jax.ShapeDtypeStruct((2, 16, SIDE, SIDE), BF)
    return pl.pallas_call(
        forward_kernel,
        in_specs=[sspec()] + [pl.BlockSpec(memory_space=pl.ANY)] * 16 + [vspec()] * 2,
        out_specs=[vspec()] * 8,
        out_shape=[hid, hid, tok, tok, turned, turned, part, part],
        scratch_shapes=[pltpu.SemaphoreType.DMA],
        compiler_params=params(16),
        cost_estimate=pl.CostEstimate(flops=3 << 30, bytes_accessed=22 << 20, transcendentals=1 << 18),
        name="forward",
    )(where, *shards, wu, wd)


REST = ((1, 16, 16), (3, 0, 16), (1, 0, 16), (3, 16, 16), (0, 0, 32))


def rest_kernel(where, x_ref, dy_ref, dt_ref, ht_ref, *outs):
    fill_parts(where, x_ref, dy_ref, dt_ref, ht_ref, outs, REST)


def rest_parts(where, x, dy, dt, ht):
    return pl.pallas_call(
        rest_kernel,
        in_specs=[sspec()] + [vspec()] * 4,
        out_specs=[vspec()] * len(REST),
        out_shape=[jax.ShapeDtypeStruct((2, n, SIDE, SIDE), BF) for _, _, n in REST],
        compiler_params=params(16),
        cost_estimate=pl.CostEstimate(flops=1 << 30, bytes_accessed=9 << 20, transcendentals=0),
        name="rest_parts",
    )(where, x, dy, dt, ht)


def ring_slot(away1, place):
    away2, near = ((2, 0), (1, 4), (2, 4), (3, 0), (1, 0), (3, 4), (0, 0), (0, 4))[place // 4]
    c = lax.axis_index("c")
    away_x = away1 + c * (away2 - away1)
    away_y = away2 + c * (away1 - away2)
    y = lax.rem(lax.axis_index("y") + away_y, 4)
    x = lax.rem(lax.axis_index("x") + away_x, 4)
    return (y * 4 + x) * 8 + near + place % 4


def token_kernel(h_ref, d_ref, wu_ref, wd_ref, send_ref, keep_ref):
    wide = 2 * SIDE
    c = lax.axis_index("c")
    for out, core in ((send_ref, 1 - c), (keep_ref, c)):
        for k in range(8):
            at = lanes(2 * k + core, wide)
            out[k, 0] = nn(h_ref[...], wd_ref[:, at]).astype(BF)
            out[k, 1] = nt(d_ref[...], wu_ref[at, :]).astype(BF)


def token_parts(h, d, wu, wd):
    part = jax.ShapeDtypeStruct((8, 2, SIDE, 2 * SIDE), BF)
    return pl.pallas_call(
        token_kernel,
        in_specs=[vspec()] * 4,
        out_specs=[vspec()] * 2,
        out_shape=[part] * 2,
        compiler_params=params(16),
        cost_estimate=pl.CostEstimate(flops=2 << 30, bytes_accessed=19 << 20, transcendentals=0),
        name="token_parts",
    )(h, d, wu, wd)


def ring(n, by):
    return [(i, (i + by) % n) for i in range(n)]


def step_both(x):
    pairs = []
    for z in range(8):
        pairs.append((z * 2, ((z + 1) % 8) * 2))
        pairs.append((z * 2 + 1, ((z - 1) % 8) * 2 + 1))
    return lax.ppermute(x, ("z", "c"), pairs)


def swap(x):
    return lax.ppermute(x, "c", [(0, 1), (1, 0)])


def add(*parts):
    total = parts[0].astype(F32)
    for p in parts[1:]:
        total = total + p.astype(F32)
    return total


def gather_over_tile(own, wu, wd):
    first, second = own, swap(own)
    shards = [first, second]
    for k in range(1, 5):
        if k == 3:
            first, wu = lax.optimization_barrier((first, wu))
        if k == 4:
            first, wd = lax.optimization_barrier((first, wd))
        first = step_both(first)
        shards += [first, swap(first)]
        if k < 4:
            second = step_both(second)
            shards += [second, swap(second)]
    return shards, wu, wd


def hop(t, stage, by):
    pairs = []
    for y in range(4):
        for x in range(4):
            for c in range(2):
                along_x = (stage + c) % 2 == 0
                to_y = y if along_x else (y + by) % 4
                to_x = (x + by) % 4 if along_x else x
                pairs.append(((y * 4 + x) * 2 + c, (to_y * 4 + to_x) * 2 + c))
    return lax.ppermute(t, ("y", "x", "c"), pairs)


def ring_sums(far_a, far_b, next_b, before_a, next_a, before_b, own):
    from_left = hop(far_a, 0, 1)
    from_right = hop(far_b, 0, -1)
    left_b = hop(next_b, 0, 1)
    right_a = hop(before_a, 0, -1)
    left_a = hop(add(next_a, from_left).astype(BF), 0, 1)
    right_b = hop(add(before_b, from_right).astype(BF), 0, -1)
    left_a, left_b, right_a, right_b = lax.optimization_barrier((left_a, left_b, right_a, right_b))

    def total(k, n):
        left, right = (left_a, right_a) if k < 16 else (left_b, right_b)
        at = slice(k % 16, k % 16 + n)
        return add(own[:, k : k + n], left[:, at], right[:, at])

    from_left = hop(total(0, 8).astype(BF), 1, 1)
    from_right = hop(total(8, 8).astype(BF), 1, -1)
    end_a = hop(add(total(16, 4), from_left[:, :4]).astype(BF), 1, 1)
    end_b = hop(add(total(20, 4), from_right[:, :4]).astype(BF), 1, -1)
    return (own, left_b, right_b, from_left, from_right, end_a, end_b)


def finish_kernel(count_ref, own, left_b, right_b, from_left, from_right, end_a, end_b, up_out, down_out):
    first = lax.axis_index(("y", "x")) * 8
    for k in range(2):
        for s in range(8):
            one, two = (end_a[k, s], from_right[k, 4 + s]) if s < 4 else (from_left[k, s], end_b[k, s - 4])
            total = add(own[k, s], left_b[k, s], right_b[k, s], one, two)
            total = jnp.where(first + s < count_ref[0], total * (1.0 / 16), 0.0)
            if k == 0:
                up_out[0, s] = total.T
            else:
                down_out[0, s] = total


def finish(count, sums):
    shape = (1, 8, SIDE, SIDE)

    def last(block):
        return pl.BlockSpec((2, 8, SIDE, SIDE), lambda i: (0, block, 0, 0))

    return pl.pallas_call(
        finish_kernel,
        grid=(1,),
        in_specs=[sspec(), last(3), last(1), last(1)] + [whole(2, n, SIDE, SIDE) for n in (8, 8, 4, 4)],
        out_specs=[whole(*shape)] * 2,
        out_shape=[jax.ShapeDtypeStruct(shape, F32)] * 2,
        compiler_params=params(16),
        cost_estimate=pl.CostEstimate(flops=1 << 20, bytes_accessed=3 << 20, transcendentals=0),
        name="finish",
    )(count, *sums)


def body(tokens, grad_out, up_tiles, down_tiles, tile_rows, tile_cols, tile_count):
    where = tile_rows[0] * COLS + tile_cols[0]
    wu = dense(where, tile_count, up_tiles, True)
    wd = dense(where, tile_count, down_tiles, False)
    shards, wu, wd = gather_over_tile(jnp.stack([tokens, grad_out]), wu, wd)
    h, d, x, dy, dt, ht, *far = forward(where, shards, wu, wd)
    rest = rest_parts(where, x, dy, dt, ht)
    h, d, _ = lax.optimization_barrier((h, d, rest[0]))
    send, keep = token_parts(h, d, wu, wd)
    pieces = add(keep, swap(send)).astype(BF)
    sums = ring_sums(*far, *rest)
    both = lax.psum_scatter(pieces, "z", scatter_dimension=0, tiled=True)[0]
    grad_up, grad_down = finish(tile_count, sums)
    return both[0], both[1], grad_up, grad_down


def solution(mesh):
    grid = Mesh(mesh.devices.reshape(4, 4, 8, 2), ("y", "x", "z", "c"))
    dp, tile = ("y", "x"), ("z", "c")
    placed = (
        P(dp, tile),
        P(dp, tile),
        P(tile, None, None, None),
        P(tile, None, None, None),
        P(tile, None),
        P(tile, None),
        P(tile),
    )
    return jax.shard_map(
        body,
        mesh=grid,
        in_specs=placed,
        out_specs=(P(dp, tile), P(dp, tile), P(tile, dp, None, None), P(tile, dp, None, None)),
        check_vma=False,
    )
```

```python
import functools

import jax
import jax.numpy as jnp
from jax import lax
from jax.experimental import pallas as pl
from jax.experimental.pallas import tpu as pltpu
from jax.sharding import Mesh, PartitionSpec as P

SIDE = 128
COLS = 32
ROWS = 8
VM = pltpu.VMEM
SM = pltpu.SMEM
BF = jnp.bfloat16
F32 = jnp.float32


def whole(*shape):
    return pl.BlockSpec(shape, lambda *i: (0,) * len(shape))


def vspec():
    return pl.BlockSpec(memory_space=VM)


def params(mib):
    return pltpu.CompilerParams(vmem_limit_bytes=mib << 20)


def sspec():
    return pl.BlockSpec(memory_space=SM)


def nn(a, b):
    return jnp.dot(a, b, preferred_element_type=F32)


def nt(a, b):
    return lax.dot_general(a, b, (((1,), (1,)), ((), ())), preferred_element_type=F32)


def gelu_pair(pre):
    curve = lax.erf(pre * 0.7071067811865476)
    value = 0.5 * pre * (1.0 + curve)
    slope = 0.5 * (1.0 + curve) + pre * jnp.exp(-0.5 * pre * pre) * 0.3989422804014327
    return value, slope


def other_owner(k):
    z, c = lax.axis_index("z"), lax.axis_index("c")
    ahead = 2 * c - 1
    if k < 2:
        return z * 2 + (c if k == 0 else 1 - c)
    hop = (k - 2) // 4 + 1
    kind = (k - 2) % 4
    chip = z + hop * ahead if kind in (0, 2) else z - hop * ahead
    core = c if kind in (0, 3) else 1 - c
    return lax.rem(chip + 8, 8) * 2 + core


def split(code):
    return code // COLS, lax.rem(code, COLS)


def dense_kernel(up, where, count_ref, tiles_ref, out_ref, sem):
    count = count_ref[0]
    out_ref[...] = jnp.zeros_like(out_ref)

    def copy(s):
        row, col = (lanes(k, SIDE) for k in split(where[s]))
        at = (col, row) if up else (row, col)
        return pltpu.make_async_copy(tiles_ref.at[0, s], out_ref.at[at], sem)

    @pl.loop(0, count)
    def _(s):
        copy(s).start()

    @pl.loop(0, count)
    def _(s):
        copy(s).wait()


def dense(where, count, tiles, up):
    features, hidden = COLS * SIDE, ROWS * SIDE
    return pl.pallas_call(
        functools.partial(dense_kernel, up),
        in_specs=[sspec()] * 2 + [pl.BlockSpec(memory_space=pltpu.HBM)],
        out_specs=vspec(),
        out_shape=jax.ShapeDtypeStruct((features, hidden) if up else (hidden, features), BF),
        scratch_shapes=[pltpu.SemaphoreType.DMA],
        compiler_params=params(16),
        cost_estimate=pl.CostEstimate(flops=0, bytes_accessed=12 << 20, transcendentals=0),
        name="dense_up" if up else "dense_down",
    )(where, count, tiles)


def lanes(k, n):
    return pl.ds(pl.multiple_of(k * n, n), n)


def forward_kernel(where, *refs):
    shards = refs[:16]
    wu_ref, wd_ref, h_ref, d_ref, x_ref, dy_ref, dt_ref, ht_ref = refs[16:24]
    parts, sem = refs[24:26], refs[26]
    wide = 2 * SIDE
    copies = []
    for k in range(16):
        at = lanes(other_owner(k), wide)
        copies.append(pltpu.make_async_copy(shards[k].at[0], x_ref.at[:, at], sem))
        copies.append(pltpu.make_async_copy(shards[k].at[1], dy_ref.at[:, at], sem))
    for copy in copies:
        copy.start()
    for copy in copies:
        copy.wait()

    @pl.loop(0, ROWS // 2)
    def _(n):
        at = lanes(n, wide)
        pre = nn(x_ref[...], wu_ref[:, at])
        grad_hidden = nt(dy_ref[...], wd_ref[at, :])
        value, slope = gelu_pair(pre)
        grad = grad_hidden * slope
        h_ref[:, at] = value.astype(BF)
        d_ref[:, at] = grad.astype(BF)
        for b in range(2):
            half = slice(b * SIDE, (b + 1) * SIDE)
            ht_ref[2 * n + b] = value[:, half].T.astype(BF)
            dt_ref[2 * n + b] = grad[:, half].T.astype(BF)

    fill_parts(where, x_ref, dy_ref, dt_ref, ht_ref, parts, ((2, 0, 16), (2, 16, 16)))


def fill_parts(where, x_ref, dy_ref, dt_ref, ht_ref, outs, blocks):
    for out, (away, start, n) in zip(outs, blocks):
        for s in range(n):
            row, col = split(where[ring_slot(away, start + s)])
            at = lanes(col, SIDE)
            out[0, s] = nn(dt_ref[row], x_ref[:, at]).astype(BF)
            out[1, s] = nn(ht_ref[row], dy_ref[:, at]).astype(BF)


def forward(where, shards, wu, wd):
    hid = jax.ShapeDtypeStruct((SIDE, ROWS * SIDE), BF)
    tok = jax.ShapeDtypeStruct((SIDE, COLS * SIDE), BF)
    turned = jax.ShapeDtypeStruct((ROWS, SIDE, SIDE), BF)
    part = jax.ShapeDtypeStruct((2, 16, SIDE, SIDE), BF)
    return pl.pallas_call(
        forward_kernel,
        in_specs=[sspec()] + [pl.BlockSpec(memory_space=pl.ANY)] * 16 + [vspec()] * 2,
        out_specs=[vspec()] * 8,
        out_shape=[hid, hid, tok, tok, turned, turned, part, part],
        scratch_shapes=[pltpu.SemaphoreType.DMA],
        compiler_params=params(16),
        cost_estimate=pl.CostEstimate(flops=3 << 30, bytes_accessed=22 << 20, transcendentals=1 << 18),
        name="forward",
    )(where, *shards, wu, wd)


REST = ((1, 16, 16), (3, 0, 16), (1, 0, 16), (3, 16, 16), (0, 0, 32))


def rest_kernel(where, x_ref, dy_ref, dt_ref, ht_ref, *outs):
    fill_parts(where, x_ref, dy_ref, dt_ref, ht_ref, outs, REST)


def rest_parts(where, x, dy, dt, ht):
    return pl.pallas_call(
        rest_kernel,
        in_specs=[sspec()] + [vspec()] * 4,
        out_specs=[vspec()] * len(REST),
        out_shape=[jax.ShapeDtypeStruct((2, n, SIDE, SIDE), BF) for _, _, n in REST],
        compiler_params=params(16),
        cost_estimate=pl.CostEstimate(flops=1 << 30, bytes_accessed=9 << 20, transcendentals=0),
        name="rest_parts",
    )(where, x, dy, dt, ht)


def ring_slot(away1, place):
    away2, near = ((2, 0), (1, 4), (2, 4), (3, 0), (1, 0), (3, 4), (0, 0), (0, 4))[place // 4]
    c = lax.axis_index("c")
    away_x = away1 + c * (away2 - away1)
    away_y = away2 + c * (away1 - away2)
    y = lax.rem(lax.axis_index("y") + away_y, 4)
    x = lax.rem(lax.axis_index("x") + away_x, 4)
    return (y * 4 + x) * 8 + near + place % 4


def token_kernel(h_ref, d_ref, wu_ref, wd_ref, send_ref, keep_ref):
    wide = 2 * SIDE
    c = lax.axis_index("c")
    for out, core in ((send_ref, 1 - c), (keep_ref, c)):
        for k in range(8):
            at = lanes(2 * k + core, wide)
            out[k, 0] = nn(h_ref[...], wd_ref[:, at]).astype(BF)
            out[k, 1] = nt(d_ref[...], wu_ref[at, :]).astype(BF)


def token_parts(h, d, wu, wd):
    part = jax.ShapeDtypeStruct((8, 2, SIDE, 2 * SIDE), BF)
    return pl.pallas_call(
        token_kernel,
        in_specs=[vspec()] * 4,
        out_specs=[vspec()] * 2,
        out_shape=[part] * 2,
        compiler_params=params(16),
        cost_estimate=pl.CostEstimate(flops=2 << 30, bytes_accessed=19 << 20, transcendentals=0),
        name="token_parts",
    )(h, d, wu, wd)


def ring(n, by):
    return [(i, (i + by) % n) for i in range(n)]


def step_both(x):
    pairs = []
    for z in range(8):
        pairs.append((z * 2, ((z + 1) % 8) * 2))
        pairs.append((z * 2 + 1, ((z - 1) % 8) * 2 + 1))
    return lax.ppermute(x, ("z", "c"), pairs)


def swap(x):
    return lax.ppermute(x, "c", [(0, 1), (1, 0)])


def add(*parts):
    total = parts[0].astype(F32)
    for p in parts[1:]:
        total = total + p.astype(F32)
    return total


def gather_over_tile(own, wu, wd):
    first, second = own, swap(own)
    shards = [first, second]
    for k in range(1, 5):
        if k == 3:
            first, wu = lax.optimization_barrier((first, wu))
        first = step_both(first)
        shards += [first, swap(first)]
        if k == 3:
            second, wd = lax.optimization_barrier((second, wd))
        if k < 4:
            second = step_both(second)
            shards += [second, swap(second)]
    return shards, wu, wd


def hop(t, stage, by):
    pairs = []
    for y in range(4):
        for x in range(4):
            for c in range(2):
                along_x = (stage + c) % 2 == 0
                to_y = y if along_x else (y + by) % 4
                to_x = (x + by) % 4 if along_x else x
                pairs.append(((y * 4 + x) * 2 + c, (to_y * 4 + to_x) * 2 + c))
    return lax.ppermute(t, ("y", "x", "c"), pairs)


def ring_sums(far_a, far_b, next_b, before_a, next_a, before_b, own, terms):
    from_left = hop(far_a, 0, 1)
    from_right = hop(far_b, 0, -1)
    left_b = hop(next_b, 0, 1)
    right_a = hop(before_a, 0, -1)
    left_a = hop(add(next_a, from_left).astype(BF), 0, 1)
    right_b = hop(add(before_b, from_right).astype(BF), 0, -1)
    left_a, left_b, right_a, right_b = lax.optimization_barrier((left_a, left_b, right_a, right_b))

    def total(k, n):
        left, right = (left_a, right_a) if k < 16 else (left_b, right_b)
        at = slice(k % 16, k % 16 + n)
        return add(own[:, k : k + n], left[:, at], right[:, at])

    from_left = hop(total(0, 8).astype(BF), 1, 1)
    from_right = hop(total(8, 8).astype(BF), 1, -1)
    from_left, from_right, terms = lax.optimization_barrier((from_left, from_right, terms))
    end_a = hop(add(total(16, 4), from_left[:, :4]).astype(BF), 1, 1)
    end_b = hop(add(total(20, 4), from_right[:, :4]).astype(BF), 1, -1)
    return (own, left_b, right_b, from_left, from_right, end_a, end_b), terms


def finish_kernel(count_ref, own, left_b, right_b, from_left, from_right, end_a, end_b, up_out, down_out):
    first = lax.axis_index(("y", "x")) * 8
    for k in range(2):
        for s in range(8):
            one, two = (end_a[k, s], from_right[k, 4 + s]) if s < 4 else (from_left[k, s], end_b[k, s - 4])
            total = add(own[k, s], left_b[k, s], right_b[k, s], one, two)
            total = jnp.where(first + s < count_ref[0], total * (1.0 / 16), 0.0)
            if k == 0:
                up_out[0, s] = total.T
            else:
                down_out[0, s] = total


def finish(count, sums):
    shape = (1, 8, SIDE, SIDE)

    def last(block):
        return pl.BlockSpec((2, 8, SIDE, SIDE), lambda i: (0, block, 0, 0))

    return pl.pallas_call(
        finish_kernel,
        grid=(1,),
        in_specs=[sspec(), last(3), last(1), last(1)] + [whole(2, n, SIDE, SIDE) for n in (8, 8, 4, 4)],
        out_specs=[whole(*shape)] * 2,
        out_shape=[jax.ShapeDtypeStruct(shape, F32)] * 2,
        compiler_params=params(16),
        cost_estimate=pl.CostEstimate(flops=1 << 20, bytes_accessed=3 << 20, transcendentals=0),
        name="finish",
    )(count, *sums)


def owner_sum_kernel(terms_ref, mixed_ref, grad_in_ref):
    for k, out in enumerate((mixed_ref, grad_in_ref)):
        total = terms_ref[0, k].astype(F32)
        for z in range(1, 8):
            total = total + terms_ref[z, k].astype(F32)
        out[...] = total.astype(BF)


def owner_sum(terms):
    shape = terms.shape[2:]
    return pl.pallas_call(
        owner_sum_kernel,
        grid=(1,),
        in_specs=[whole(*terms.shape)],
        out_specs=[whole(*shape)] * 2,
        out_shape=[jax.ShapeDtypeStruct(shape, BF)] * 2,
        compiler_params=params(16),
        cost_estimate=pl.CostEstimate(flops=1 << 19, bytes_accessed=1 << 20, transcendentals=0),
        name="owner_sum",
    )(terms)


def body(tokens, grad_out, up_tiles, down_tiles, tile_rows, tile_cols, tile_count):
    where = tile_rows[0] * COLS + tile_cols[0]
    wu = dense(where, tile_count, up_tiles, True)
    wd = dense(where, tile_count, down_tiles, False)
    shards, wu, wd = gather_over_tile(jnp.stack([tokens, grad_out]), wu, wd)
    h, d, x, dy, dt, ht, *far = forward(where, shards, wu, wd)
    rest = rest_parts(where, x, dy, dt, ht)
    h, d, _ = lax.optimization_barrier((h, d, rest[0]))
    send, keep = token_parts(h, d, wu, wd)
    pieces = add(keep, swap(send)).astype(BF)
    terms = lax.all_to_all(pieces, "z", 0, 0, tiled=True)
    sums, terms = ring_sums(*far, *rest, terms)
    grad_up, grad_down = finish(tile_count, sums)
    mixed, grad_in = owner_sum(terms)
    return mixed, grad_in, grad_up, grad_down


def solution(mesh):
    grid = Mesh(mesh.devices.reshape(4, 4, 8, 2), ("y", "x", "z", "c"))
    dp, tile = ("y", "x"), ("z", "c")
    placed = (
        P(dp, tile),
        P(dp, tile),
        P(tile, None, None, None),
        P(tile, None, None, None),
        P(tile, None),
        P(tile, None),
        P(tile),
    )
    return jax.shard_map(
        body,
        mesh=grid,
        in_specs=placed,
        out_specs=(P(dp, tile), P(dp, tile), P(tile, dp, None, None), P(tile, dp, None, None)),
        check_vma=False,
    )
```

```python
import functools

import jax
import jax.numpy as jnp
from jax import lax
from jax.experimental import pallas as pl
from jax.experimental.pallas import tpu as pltpu
from jax.sharding import Mesh, PartitionSpec as P

SIDE = 128
COLS = 32
ROWS = 8
VM = pltpu.VMEM
SM = pltpu.SMEM
BF = jnp.bfloat16
F32 = jnp.float32


def whole(*shape):
    return pl.BlockSpec(shape, lambda *i: (0,) * len(shape))


def vspec():
    return pl.BlockSpec(memory_space=VM)


def params(mib):
    return pltpu.CompilerParams(vmem_limit_bytes=mib << 20)


def sspec():
    return pl.BlockSpec(memory_space=SM)


def nn(a, b):
    return jnp.dot(a, b, preferred_element_type=F32)


def nt(a, b):
    return lax.dot_general(a, b, (((1,), (1,)), ((), ())), preferred_element_type=F32)


def gelu_pair(pre):
    curve = lax.erf(pre * 0.7071067811865476)
    value = 0.5 * pre * (1.0 + curve)
    slope = 0.5 * (1.0 + curve) + pre * jnp.exp(-0.5 * pre * pre) * 0.3989422804014327
    return value, slope


def other_owner(k):
    z, c = lax.axis_index("z"), lax.axis_index("c")
    ahead = 2 * c - 1
    if k < 2:
        return z * 2 + (c if k == 0 else 1 - c)
    hop = (k - 2) // 4 + 1
    kind = (k - 2) % 4
    chip = z + hop * ahead if kind in (0, 2) else z - hop * ahead
    core = c if kind in (0, 3) else 1 - c
    return lax.rem(chip + 8, 8) * 2 + core


def split(code):
    return code // COLS, lax.rem(code, COLS)


def dense_kernel(up, where, count_ref, tiles_ref, out_ref, sem):
    count = count_ref[0]
    out_ref[...] = jnp.zeros_like(out_ref)

    def copy(s):
        row, col = (lanes(k, SIDE) for k in split(where[s]))
        at = (col, row) if up else (row, col)
        return pltpu.make_async_copy(tiles_ref.at[0, s], out_ref.at[at], sem)

    @pl.loop(0, count)
    def _(s):
        copy(s).start()

    @pl.loop(0, count)
    def _(s):
        copy(s).wait()


def dense(where, count, tiles, up):
    features, hidden = COLS * SIDE, ROWS * SIDE
    return pl.pallas_call(
        functools.partial(dense_kernel, up),
        in_specs=[sspec()] * 2 + [pl.BlockSpec(memory_space=pltpu.HBM)],
        out_specs=vspec(),
        out_shape=jax.ShapeDtypeStruct((features, hidden) if up else (hidden, features), BF),
        scratch_shapes=[pltpu.SemaphoreType.DMA],
        compiler_params=params(16),
        cost_estimate=pl.CostEstimate(flops=0, bytes_accessed=12 << 20, transcendentals=0),
        name="dense_up" if up else "dense_down",
    )(where, count, tiles)


def lanes(k, n):
    return pl.ds(pl.multiple_of(k * n, n), n)


EARLY = 10


def early_kernel(*refs):
    shards, (wu_ref, wd_ref, pre_ref, gh_ref, x_ref, dy_ref, sem) = refs[:EARLY], refs[EARLY:]
    fetch_shards(shards, range(EARLY), x_ref, dy_ref, sem)
    wide = 2 * SIDE
    for n in range(ROWS // 2):
        at = slice(n * wide, (n + 1) * wide)
        pre_ref[:, at], gh_ref[:, at] = products(range(EARLY), at, x_ref, dy_ref, wu_ref, wd_ref)


def fetch_shards(shards, which, x_ref, dy_ref, sem):
    copies = []
    for k in which:
        at = lanes(other_owner(k), 2 * SIDE)
        copies.append(pltpu.make_async_copy(shards[k].at[0], x_ref.at[:, at], sem))
        copies.append(pltpu.make_async_copy(shards[k].at[1], dy_ref.at[:, at], sem))
    for copy in copies:
        copy.start()
    for copy in copies:
        copy.wait()


def products(which, at, x_ref, dy_ref, wu_ref, wd_ref):
    pre, grad_hidden = 0.0, 0.0
    for k in which:
        features = lanes(other_owner(k), 2 * SIDE)
        pre = pre + nn(x_ref[:, features], wu_ref[features, at])
        grad_hidden = grad_hidden + nt(dy_ref[:, features], wd_ref[at, features])
    return pre, grad_hidden


def early(shards, wu, wd):
    acc = jax.ShapeDtypeStruct((SIDE, ROWS * SIDE), F32)
    return pl.pallas_call(
        early_kernel,
        in_specs=[pl.BlockSpec(memory_space=pl.ANY)] * EARLY + [vspec()] * 2,
        out_specs=[vspec()] * 2,
        out_shape=[acc, acc],
        scratch_shapes=[VM((SIDE, COLS * SIDE), BF)] * 2 + [pltpu.SemaphoreType.DMA],
        compiler_params=params(16),
        cost_estimate=pl.CostEstimate(flops=5 << 28, bytes_accessed=13 << 20, transcendentals=0),
        name="early",
    )(*shards[:EARLY], wu, wd)


def forward_kernel(where, *refs):
    shards = refs[:16]
    wu_ref, wd_ref, pre_ref, gh_ref = refs[16:20]
    h_ref, d_ref, x_ref, dy_ref, dt_ref, ht_ref = refs[20:26]
    parts, sem = refs[26:28], refs[28]
    wide = 2 * SIDE
    fetch_shards(shards, range(16), x_ref, dy_ref, sem)
    for n in range(ROWS // 2):
        at = slice(n * wide, (n + 1) * wide)
        pre, grad_hidden = products(range(EARLY, 16), at, x_ref, dy_ref, wu_ref, wd_ref)
        value, slope = gelu_pair(pre + pre_ref[:, at])
        grad = (grad_hidden + gh_ref[:, at]) * slope
        h_ref[:, at] = value.astype(BF)
        d_ref[:, at] = grad.astype(BF)
        for b in range(2):
            half = slice(b * SIDE, (b + 1) * SIDE)
            ht_ref[2 * n + b] = value[:, half].T.astype(BF)
            dt_ref[2 * n + b] = grad[:, half].T.astype(BF)
    fill_parts(where, x_ref, dy_ref, dt_ref, ht_ref, parts, ((2, 0, 16), (2, 16, 16)))


def fill_parts(where, x_ref, dy_ref, dt_ref, ht_ref, outs, blocks):
    for out, (away, start, n) in zip(outs, blocks):
        for s in range(n):
            row, col = split(where[ring_slot(away, start + s)])
            at = lanes(col, SIDE)
            out[0, s] = nn(dt_ref[row], x_ref[:, at]).astype(BF)
            out[1, s] = nn(ht_ref[row], dy_ref[:, at]).astype(BF)


def forward(where, shards, wu, wd, first):
    hid = jax.ShapeDtypeStruct((SIDE, ROWS * SIDE), BF)
    tok = jax.ShapeDtypeStruct((SIDE, COLS * SIDE), BF)
    turned = jax.ShapeDtypeStruct((ROWS, SIDE, SIDE), BF)
    part = jax.ShapeDtypeStruct((2, 16, SIDE, SIDE), BF)
    return pl.pallas_call(
        forward_kernel,
        in_specs=[sspec()] + [pl.BlockSpec(memory_space=pl.ANY)] * 16 + [vspec()] * 4,
        out_specs=[vspec()] * 8,
        out_shape=[hid, hid, tok, tok, turned, turned, part, part],
        scratch_shapes=[pltpu.SemaphoreType.DMA],
        compiler_params=params(16),
        cost_estimate=pl.CostEstimate(flops=3 << 30, bytes_accessed=22 << 20, transcendentals=1 << 18),
        name="forward",
    )(where, *shards, wu, wd, *first)


REST = ((1, 16, 16), (3, 0, 16), (1, 0, 16), (3, 16, 16), (0, 0, 32))


def rest_kernel(where, x_ref, dy_ref, dt_ref, ht_ref, *outs):
    fill_parts(where, x_ref, dy_ref, dt_ref, ht_ref, outs, REST)


def rest_parts(where, x, dy, dt, ht):
    return pl.pallas_call(
        rest_kernel,
        in_specs=[sspec()] + [vspec()] * 4,
        out_specs=[vspec()] * len(REST),
        out_shape=[jax.ShapeDtypeStruct((2, n, SIDE, SIDE), BF) for _, _, n in REST],
        compiler_params=params(16),
        cost_estimate=pl.CostEstimate(flops=1 << 30, bytes_accessed=9 << 20, transcendentals=0),
        name="rest_parts",
    )(where, x, dy, dt, ht)


def ring_slot(away1, place):
    away2, near = ((2, 0), (1, 4), (2, 4), (3, 0), (1, 0), (3, 4), (0, 0), (0, 4))[place // 4]
    c = lax.axis_index("c")
    away_x = away1 + c * (away2 - away1)
    away_y = away2 + c * (away1 - away2)
    y = lax.rem(lax.axis_index("y") + away_y, 4)
    x = lax.rem(lax.axis_index("x") + away_x, 4)
    return (y * 4 + x) * 8 + near + place % 4


def token_kernel(h_ref, d_ref, wu_ref, wd_ref, send_ref, keep_ref):
    wide = 2 * SIDE
    c = lax.axis_index("c")
    for out, core in ((send_ref, 1 - c), (keep_ref, c)):
        for k in range(8):
            at = lanes(2 * k + core, wide)
            out[k, 0] = nn(h_ref[...], wd_ref[:, at]).astype(BF)
            out[k, 1] = nt(d_ref[...], wu_ref[at, :]).astype(BF)


def token_parts(h, d, wu, wd):
    part = jax.ShapeDtypeStruct((8, 2, SIDE, 2 * SIDE), BF)
    return pl.pallas_call(
        token_kernel,
        in_specs=[vspec()] * 4,
        out_specs=[vspec()] * 2,
        out_shape=[part] * 2,
        compiler_params=params(16),
        cost_estimate=pl.CostEstimate(flops=2 << 30, bytes_accessed=19 << 20, transcendentals=0),
        name="token_parts",
    )(h, d, wu, wd)


def ring(n, by):
    return [(i, (i + by) % n) for i in range(n)]


def step_both(x):
    pairs = []
    for z in range(8):
        pairs.append((z * 2, ((z + 1) % 8) * 2))
        pairs.append((z * 2 + 1, ((z - 1) % 8) * 2 + 1))
    return lax.ppermute(x, ("z", "c"), pairs)


def swap(x):
    return lax.ppermute(x, "c", [(0, 1), (1, 0)])


def add(*parts):
    total = parts[0].astype(F32)
    for p in parts[1:]:
        total = total + p.astype(F32)
    return total


def gather_over_tile(own, wu, wd):
    first, second = own, swap(own)
    shards = [first, second]
    for k in range(1, 5):
        if k == 3:
            first, wu = lax.optimization_barrier((first, wu))
        first = step_both(first)
        if k == 4:
            sums = early(shards, wu, wd)
            first, *sums = lax.optimization_barrier((first, *sums))
        shards += [first, swap(first)]
        if k == 3:
            second, wd = lax.optimization_barrier((second, wd))
        if k < 4:
            second = step_both(second)
            shards += [second, swap(second)]
    return shards, wu, wd, sums


def hop(t, stage, by):
    pairs = []
    for y in range(4):
        for x in range(4):
            for c in range(2):
                along_x = (stage + c) % 2 == 0
                to_y = y if along_x else (y + by) % 4
                to_x = (x + by) % 4 if along_x else x
                pairs.append(((y * 4 + x) * 2 + c, (to_y * 4 + to_x) * 2 + c))
    return lax.ppermute(t, ("y", "x", "c"), pairs)


def ring_sums(far_a, far_b, next_b, before_a, next_a, before_b, own, terms):
    from_left = hop(far_a, 0, 1)
    from_right = hop(far_b, 0, -1)
    left_b = hop(next_b, 0, 1)
    right_a = hop(before_a, 0, -1)
    left_a = hop(add(next_a, from_left).astype(BF), 0, 1)
    right_b = hop(add(before_b, from_right).astype(BF), 0, -1)
    left_a, left_b, right_a, right_b = lax.optimization_barrier((left_a, left_b, right_a, right_b))

    def total(k, n):
        left, right = (left_a, right_a) if k < 16 else (left_b, right_b)
        at = slice(k % 16, k % 16 + n)
        return add(own[:, k : k + n], left[:, at], right[:, at])

    from_left = hop(total(0, 8).astype(BF), 1, 1)
    from_right = hop(total(8, 8).astype(BF), 1, -1)
    from_left, terms = lax.optimization_barrier((from_left, terms))
    end_a = hop(add(total(16, 4), from_left[:, :4]).astype(BF), 1, 1)
    end_b = hop(add(total(20, 4), from_right[:, :4]).astype(BF), 1, -1)
    return (near_sum(own, left_b, right_b), from_left, from_right, end_a, end_b), terms


def near_sum_kernel(own, left_b, right_b, out):
    for k in range(2):
        for s in range(8):
            out[k, s] = add(own[k, s], left_b[k, s], right_b[k, s])


def near_sum(own, left_b, right_b):
    def last(block):
        return pl.BlockSpec((2, 8, SIDE, SIDE), lambda i: (0, block, 0, 0))

    return pl.pallas_call(
        near_sum_kernel,
        grid=(1,),
        in_specs=[last(3), last(1), last(1)],
        out_specs=whole(2, 8, SIDE, SIDE),
        out_shape=jax.ShapeDtypeStruct((2, 8, SIDE, SIDE), F32),
        compiler_params=params(16),
        cost_estimate=pl.CostEstimate(flops=1 << 19, bytes_accessed=3 << 20, transcendentals=0),
        name="near_sum",
    )(own, left_b, right_b)


def finish_kernel(count_ref, near, from_left, from_right, end_a, end_b, up_out, down_out):
    first = lax.axis_index(("y", "x")) * 8
    for k in range(2):
        for s in range(8):
            one, two = (end_a[k, s], from_right[k, 4 + s]) if s < 4 else (from_left[k, s], end_b[k, s - 4])
            total = add(near[k, s], one, two)
            total = jnp.where(first + s < count_ref[0], total * (1.0 / 16), 0.0)
            if k == 0:
                up_out[0, s] = total.T
            else:
                down_out[0, s] = total


def finish(count, sums):
    shape = (1, 8, SIDE, SIDE)
    return pl.pallas_call(
        finish_kernel,
        grid=(1,),
        in_specs=[sspec()] + [whole(2, n, SIDE, SIDE) for n in (8, 8, 8, 4, 4)],
        out_specs=[whole(*shape)] * 2,
        out_shape=[jax.ShapeDtypeStruct(shape, F32)] * 2,
        compiler_params=params(16),
        cost_estimate=pl.CostEstimate(flops=1 << 20, bytes_accessed=3 << 20, transcendentals=0),
        name="finish",
    )(count, *sums)


def owner_sum_kernel(terms_ref, mixed_ref, grad_in_ref):
    for k, out in enumerate((mixed_ref, grad_in_ref)):
        total = terms_ref[0, k].astype(F32)
        for z in range(1, 8):
            total = total + terms_ref[z, k].astype(F32)
        out[...] = total.astype(BF)


def owner_sum(terms):
    shape = terms.shape[2:]
    return pl.pallas_call(
        owner_sum_kernel,
        grid=(1,),
        in_specs=[whole(*terms.shape)],
        out_specs=[whole(*shape)] * 2,
        out_shape=[jax.ShapeDtypeStruct(shape, BF)] * 2,
        compiler_params=params(16),
        cost_estimate=pl.CostEstimate(flops=1 << 19, bytes_accessed=1 << 20, transcendentals=0),
        name="owner_sum",
    )(terms)


def body(tokens, grad_out, up_tiles, down_tiles, tile_rows, tile_cols, tile_count):
    where = tile_rows[0] * COLS + tile_cols[0]
    wu = dense(where, tile_count, up_tiles, True)
    wd = dense(where, tile_count, down_tiles, False)
    shards, wu, wd, first = gather_over_tile(jnp.stack([tokens, grad_out]), wu, wd)
    h, d, x, dy, dt, ht, *far = forward(where, shards, wu, wd, first)
    rest = rest_parts(where, x, dy, dt, ht)
    h, d, _ = lax.optimization_barrier((h, d, rest[0]))
    send, keep = token_parts(h, d, wu, wd)
    pieces = add(keep, swap(send)).astype(BF)
    terms = lax.all_to_all(pieces, "z", 0, 0, tiled=True)
    sums, terms = ring_sums(*far, *rest, terms)
    grad_up, grad_down = finish(tile_count, sums)
    mixed, grad_in = owner_sum(terms)
    return mixed, grad_in, grad_up, grad_down


def solution(mesh):
    grid = Mesh(mesh.devices.reshape(4, 4, 8, 2), ("y", "x", "z", "c"))
    dp, tile = ("y", "x"), ("z", "c")
    placed = (
        P(dp, tile),
        P(dp, tile),
        P(tile, None, None, None),
        P(tile, None, None, None),
        P(tile, None),
        P(tile, None),
        P(tile),
    )
    return jax.shard_map(
        body,
        mesh=grid,
        in_specs=placed,
        out_specs=(P(dp, tile), P(dp, tile), P(tile, dp, None, None), P(tile, dp, None, None)),
        check_vma=False,
    )
```

```python
import functools

import jax
import jax.numpy as jnp
from jax import lax
from jax.experimental import pallas as pl
from jax.experimental.pallas import tpu as pltpu
from jax.sharding import Mesh, PartitionSpec as P

SIDE = 128
COLS = 32
ROWS = 8
VM = pltpu.VMEM
SM = pltpu.SMEM
BF = jnp.bfloat16
F32 = jnp.float32


def whole(*shape):
    return pl.BlockSpec(shape, lambda *i: (0,) * len(shape))


def vspec():
    return pl.BlockSpec(memory_space=VM)


def params(mib):
    return pltpu.CompilerParams(vmem_limit_bytes=mib << 20)


def sspec():
    return pl.BlockSpec(memory_space=SM)


def nn(a, b):
    return jnp.dot(a, b, preferred_element_type=F32)


def nt(a, b):
    return lax.dot_general(a, b, (((1,), (1,)), ((), ())), preferred_element_type=F32)


def gelu_pair(pre):
    curve = lax.erf(pre * 0.7071067811865476)
    value = 0.5 * pre * (1.0 + curve)
    slope = 0.5 * (1.0 + curve) + pre * jnp.exp(-0.5 * pre * pre) * 0.3989422804014327
    return value, slope


def other_owner(k):
    z, c = lax.axis_index("z"), lax.axis_index("c")
    ahead = 2 * c - 1
    if k < 2:
        return z * 2 + (c if k == 0 else 1 - c)
    hop = (k - 2) // 4 + 1
    kind = (k - 2) % 4
    chip = z + hop * ahead if kind in (0, 2) else z - hop * ahead
    core = c if kind in (0, 3) else 1 - c
    return lax.rem(chip + 8, 8) * 2 + core


def split(code):
    return code // COLS, lax.rem(code, COLS)


def dense_kernel(up, where, count_ref, tiles_ref, out_ref, sem):
    count = count_ref[0]
    out_ref[...] = jnp.zeros_like(out_ref)

    def copy(s):
        row, col = (lanes(k, SIDE) for k in split(where[s]))
        at = (col, row) if up else (row, col)
        return pltpu.make_async_copy(tiles_ref.at[0, s], out_ref.at[at], sem)

    @pl.loop(0, count)
    def _(s):
        copy(s).start()

    @pl.loop(0, count)
    def _(s):
        copy(s).wait()


def dense(where, count, tiles, up):
    features, hidden = COLS * SIDE, ROWS * SIDE
    return pl.pallas_call(
        functools.partial(dense_kernel, up),
        in_specs=[sspec()] * 2 + [pl.BlockSpec(memory_space=pltpu.HBM)],
        out_specs=vspec(),
        out_shape=jax.ShapeDtypeStruct((features, hidden) if up else (hidden, features), BF),
        scratch_shapes=[pltpu.SemaphoreType.DMA],
        compiler_params=params(16),
        cost_estimate=pl.CostEstimate(flops=0, bytes_accessed=12 << 20, transcendentals=0),
        name="dense_up" if up else "dense_down",
    )(where, count, tiles)


def lanes(k, n):
    return pl.ds(pl.multiple_of(k * n, n), n)


EARLY = 10


def early_kernel(*refs):
    shards, (wu_ref, wd_ref, pre_ref, gh_ref, x_ref, dy_ref, sem) = refs[:EARLY], refs[EARLY:]
    fetch_shards(shards, range(EARLY), x_ref, dy_ref, sem)
    wide = 2 * SIDE
    for n in range(ROWS // 2):
        at = slice(n * wide, (n + 1) * wide)
        pre_ref[:, at], gh_ref[:, at] = products(range(EARLY), at, x_ref, dy_ref, wu_ref, wd_ref)


def fetch_shards(shards, which, x_ref, dy_ref, sem):
    copies = []
    for k in which:
        at = lanes(other_owner(k), 2 * SIDE)
        copies.append(pltpu.make_async_copy(shards[k].at[0], x_ref.at[:, at], sem))
        copies.append(pltpu.make_async_copy(shards[k].at[1], dy_ref.at[:, at], sem))
    for copy in copies:
        copy.start()
    for copy in copies:
        copy.wait()


def products(which, at, x_ref, dy_ref, wu_ref, wd_ref):
    pre, grad_hidden = 0.0, 0.0
    for k in which:
        features = lanes(other_owner(k), 2 * SIDE)
        pre = pre + nn(x_ref[:, features], wu_ref[features, at])
        grad_hidden = grad_hidden + nt(dy_ref[:, features], wd_ref[at, features])
    return pre, grad_hidden


def early(shards, wu, wd):
    acc = jax.ShapeDtypeStruct((SIDE, ROWS * SIDE), F32)
    return pl.pallas_call(
        early_kernel,
        in_specs=[pl.BlockSpec(memory_space=pl.ANY)] * EARLY + [vspec()] * 2,
        out_specs=[vspec()] * 2,
        out_shape=[acc, acc],
        scratch_shapes=[VM((SIDE, COLS * SIDE), BF)] * 2 + [pltpu.SemaphoreType.DMA],
        compiler_params=params(16),
        cost_estimate=pl.CostEstimate(flops=5 << 28, bytes_accessed=13 << 20, transcendentals=0),
        name="early",
    )(*shards[:EARLY], wu, wd)


def forward_kernel(where, *refs):
    shards = refs[:16]
    wu_ref, wd_ref, pre_ref, gh_ref = refs[16:20]
    h_ref, d_ref, x_ref, dy_ref, dt_ref, ht_ref = refs[20:26]
    parts, sem = refs[26:28], refs[28]
    wide = 2 * SIDE
    fetch_shards(shards, range(16), x_ref, dy_ref, sem)
    for n in range(ROWS // 2):
        at = slice(n * wide, (n + 1) * wide)
        pre, grad_hidden = products(range(EARLY, 16), at, x_ref, dy_ref, wu_ref, wd_ref)
        value, slope = gelu_pair(pre + pre_ref[:, at])
        grad = (grad_hidden + gh_ref[:, at]) * slope
        h_ref[:, at] = value.astype(BF)
        d_ref[:, at] = grad.astype(BF)
        for b in range(2):
            half = slice(b * SIDE, (b + 1) * SIDE)
            ht_ref[2 * n + b] = value[:, half].T.astype(BF)
            dt_ref[2 * n + b] = grad[:, half].T.astype(BF)
    fill_parts(where, x_ref, dy_ref, dt_ref, ht_ref, parts, ((2, 0, 16), (2, 16, 16)))


def fill_parts(where, x_ref, dy_ref, dt_ref, ht_ref, outs, blocks):
    for out, (away, start, n) in zip(outs, blocks):
        for s in range(n):
            row, col = split(where[ring_slot(away, start + s)])
            at = lanes(col, SIDE)
            out[0, s] = nn(dt_ref[row], x_ref[:, at]).astype(BF)
            out[1, s] = nn(ht_ref[row], dy_ref[:, at]).astype(BF)


def forward(where, shards, wu, wd, first):
    hid = jax.ShapeDtypeStruct((SIDE, ROWS * SIDE), BF)
    tok = jax.ShapeDtypeStruct((SIDE, COLS * SIDE), BF)
    turned = jax.ShapeDtypeStruct((ROWS, SIDE, SIDE), BF)
    part = jax.ShapeDtypeStruct((2, 16, SIDE, SIDE), BF)
    return pl.pallas_call(
        forward_kernel,
        in_specs=[sspec()] + [pl.BlockSpec(memory_space=pl.ANY)] * 16 + [vspec()] * 4,
        out_specs=[vspec()] * 8,
        out_shape=[hid, hid, tok, tok, turned, turned, part, part],
        scratch_shapes=[pltpu.SemaphoreType.DMA],
        compiler_params=params(16),
        cost_estimate=pl.CostEstimate(flops=3 << 30, bytes_accessed=22 << 20, transcendentals=1 << 18),
        name="forward",
    )(where, *shards, wu, wd, *first)


REST = ((1, 16, 16), (3, 0, 16), (1, 0, 16), (3, 16, 16), (0, 0, 32))


def rest_kernel(where, x_ref, dy_ref, dt_ref, ht_ref, *outs):
    fill_parts(where, x_ref, dy_ref, dt_ref, ht_ref, outs, REST)


def rest_parts(where, x, dy, dt, ht):
    return pl.pallas_call(
        rest_kernel,
        in_specs=[sspec()] + [vspec()] * 4,
        out_specs=[vspec()] * len(REST),
        out_shape=[jax.ShapeDtypeStruct((2, n, SIDE, SIDE), BF) for _, _, n in REST],
        compiler_params=params(16),
        cost_estimate=pl.CostEstimate(flops=1 << 30, bytes_accessed=9 << 20, transcendentals=0),
        name="rest_parts",
    )(where, x, dy, dt, ht)


def ring_slot(away1, place):
    away2, near = ((2, 0), (1, 4), (2, 4), (3, 0), (1, 0), (3, 4), (0, 0), (0, 4))[place // 4]
    c = lax.axis_index("c")
    away_x = away1 + c * (away2 - away1)
    away_y = away2 + c * (away1 - away2)
    y = lax.rem(lax.axis_index("y") + away_y, 4)
    x = lax.rem(lax.axis_index("x") + away_x, 4)
    return (y * 4 + x) * 8 + near + place % 4


def token_kernel(h_ref, d_ref, wu_ref, wd_ref, send_ref, keep_ref):
    wide = 2 * SIDE
    c = lax.axis_index("c")
    for out, core in ((send_ref, 1 - c), (keep_ref, c)):
        for k in range(8):
            at = lanes(2 * k + core, wide)
            out[k, 0] = nn(h_ref[...], wd_ref[:, at]).astype(BF)
            out[k, 1] = nt(d_ref[...], wu_ref[at, :]).astype(BF)


def token_parts(h, d, wu, wd):
    part = jax.ShapeDtypeStruct((8, 2, SIDE, 2 * SIDE), BF)
    return pl.pallas_call(
        token_kernel,
        in_specs=[vspec()] * 4,
        out_specs=[vspec()] * 2,
        out_shape=[part] * 2,
        compiler_params=params(16),
        cost_estimate=pl.CostEstimate(flops=2 << 30, bytes_accessed=19 << 20, transcendentals=0),
        name="token_parts",
    )(h, d, wu, wd)


def ring(n, by):
    return [(i, (i + by) % n) for i in range(n)]


def step_both(x):
    pairs = []
    for z in range(8):
        pairs.append((z * 2, ((z + 1) % 8) * 2))
        pairs.append((z * 2 + 1, ((z - 1) % 8) * 2 + 1))
    return lax.ppermute(x, ("z", "c"), pairs)


def swap(x):
    return lax.ppermute(x, "c", [(0, 1), (1, 0)])


def add(*parts):
    total = parts[0].astype(F32)
    for p in parts[1:]:
        total = total + p.astype(F32)
    return total


def gather_over_tile(own, wu, wd):
    first, second = own, swap(own)
    shards = [first, second]
    for k in range(1, 5):
        if k == 3:
            first, wu = lax.optimization_barrier((first, wu))
        first = step_both(first)
        if k == 4:
            sums = early(shards, wu, wd)
            first, *sums = lax.optimization_barrier((first, *sums))
        shards += [first, swap(first)]
        if k == 3:
            second, wd = lax.optimization_barrier((second, wd))
        if k < 4:
            second = step_both(second)
            shards += [second, swap(second)]
    return shards, wu, wd, sums


def hop(t, stage, by):
    pairs = []
    for y in range(4):
        for x in range(4):
            for c in range(2):
                along_x = (stage + c) % 2 == 0
                to_y = y if along_x else (y + by) % 4
                to_x = (x + by) % 4 if along_x else x
                pairs.append(((y * 4 + x) * 2 + c, (to_y * 4 + to_x) * 2 + c))
    return lax.ppermute(t, ("y", "x", "c"), pairs)


def ring_sums(far_a, far_b, next_b, before_a, next_a, before_b, own, terms):
    from_left = hop(far_a, 0, 1)
    from_right = hop(far_b, 0, -1)
    left_b = hop(next_b, 0, 1)
    right_a = hop(before_a, 0, -1)
    left_a = hop(add(next_a, from_left).astype(BF), 0, 1)
    right_b = hop(add(before_b, from_right).astype(BF), 0, -1)
    left_a, left_b, right_a, right_b = lax.optimization_barrier((left_a, left_b, right_a, right_b))

    plus, minus = send_sums(own, left_a, right_a)
    from_left = hop(plus, 1, 1)
    from_right = hop(minus, 1, -1)
    mid, near = kept_sums(own, left_b, right_b)
    from_left, terms = lax.optimization_barrier((from_left, terms))
    end_a = hop(add(mid[:, :4], from_left[:, :4]).astype(BF), 1, 1)
    end_b = hop(add(mid[:, 4:], from_right[:, :4]).astype(BF), 1, -1)
    return (near_sum(near, from_left, from_right), end_a, end_b), terms


def three_sum_kernel(own, left, right, one_ref, two_ref):
    for half, out in enumerate((one_ref, two_ref)):

        @pl.when(pl.program_id(0) == half)
        def _():
            for k in range(2):
                for s in range(8):
                    out[k, s] = add(own[k, s], left[k, s], right[k, s]).astype(out.dtype)


def three_sum(own, left, right, half, dtype, name):
    block = (2, 8, SIDE, SIDE)
    return pl.pallas_call(
        three_sum_kernel,
        grid=(2,),
        in_specs=[pl.BlockSpec(block, lambda i: (0, 2 * half + i, 0, 0))]
        + [pl.BlockSpec(block, lambda i: (0, i, 0, 0))] * 2,
        out_specs=[whole(*block)] * 2,
        out_shape=[jax.ShapeDtypeStruct(block, dtype)] * 2,
        compiler_params=params(16),
        cost_estimate=pl.CostEstimate(flops=1 << 20, bytes_accessed=4 << 20, transcendentals=0),
        name=name,
    )(own, left, right)


def send_sums(own, left_a, right_a):
    return three_sum(own, left_a, right_a, 0, BF, "send_sums")


def kept_sums(own, left_b, right_b):
    return three_sum(own, left_b, right_b, 1, F32, "kept_sums")


def near_sum_kernel(near, from_left, from_right, out):
    for k in range(2):
        for s in range(4):
            out[k, s] = add(near[k, s], from_right[k, s])
            out[k, 4 + s] = add(near[k, 4 + s], from_left[k, s])


def near_sum(near, from_left, from_right):
    block = (2, 8, SIDE, SIDE)
    half = pl.BlockSpec((2, 4, SIDE, SIDE), lambda i: (0, 1, 0, 0))
    return pl.pallas_call(
        near_sum_kernel,
        grid=(1,),
        in_specs=[whole(*block), half, half],
        out_specs=whole(*block),
        out_shape=jax.ShapeDtypeStruct(block, F32),
        compiler_params=params(16),
        cost_estimate=pl.CostEstimate(flops=1 << 19, bytes_accessed=3 << 20, transcendentals=0),
        name="near_sum",
    )(near, from_left, from_right)


def finish_kernel(count_ref, near, end_a, end_b, up_out, down_out):
    first = lax.axis_index(("y", "x")) * 8
    for k in range(2):
        for s in range(8):
            total = add(near[k, s], end_a[k, s] if s < 4 else end_b[k, s - 4])
            total = jnp.where(first + s < count_ref[0], total * (1.0 / 16), 0.0)
            if k == 0:
                up_out[0, s] = total.T
            else:
                down_out[0, s] = total


def finish(count, sums):
    shape = (1, 8, SIDE, SIDE)
    return pl.pallas_call(
        finish_kernel,
        grid=(1,),
        in_specs=[sspec()] + [whole(2, n, SIDE, SIDE) for n in (8, 4, 4)],
        out_specs=[whole(*shape)] * 2,
        out_shape=[jax.ShapeDtypeStruct(shape, F32)] * 2,
        compiler_params=params(16),
        cost_estimate=pl.CostEstimate(flops=1 << 20, bytes_accessed=3 << 20, transcendentals=0),
        name="finish",
    )(count, *sums)


def owner_sum_kernel(terms_ref, mixed_ref, grad_in_ref):
    for k, out in enumerate((mixed_ref, grad_in_ref)):
        total = terms_ref[0, k].astype(F32)
        for z in range(1, 8):
            total = total + terms_ref[z, k].astype(F32)
        out[...] = total.astype(BF)


def owner_sum(terms):
    shape = terms.shape[2:]
    return pl.pallas_call(
        owner_sum_kernel,
        grid=(1,),
        in_specs=[whole(*terms.shape)],
        out_specs=[whole(*shape)] * 2,
        out_shape=[jax.ShapeDtypeStruct(shape, BF)] * 2,
        compiler_params=params(16),
        cost_estimate=pl.CostEstimate(flops=1 << 19, bytes_accessed=1 << 20, transcendentals=0),
        name="owner_sum",
    )(terms)


def body(tokens, grad_out, up_tiles, down_tiles, tile_rows, tile_cols, tile_count):
    where = tile_rows[0] * COLS + tile_cols[0]
    wu = dense(where, tile_count, up_tiles, True)
    wd = dense(where, tile_count, down_tiles, False)
    shards, wu, wd, first = gather_over_tile(jnp.stack([tokens, grad_out]), wu, wd)
    h, d, x, dy, dt, ht, *far = forward(where, shards, wu, wd, first)
    rest = rest_parts(where, x, dy, dt, ht)
    h, d, _ = lax.optimization_barrier((h, d, rest[0]))
    send, keep = token_parts(h, d, wu, wd)
    pieces = add(keep, swap(send)).astype(BF)
    terms = lax.all_to_all(pieces, "z", 0, 0, tiled=True)
    sums, terms = ring_sums(*far, *rest, terms)
    grad_up, grad_down = finish(tile_count, sums)
    mixed, grad_in = owner_sum(terms)
    return mixed, grad_in, grad_up, grad_down


def solution(mesh):
    grid = Mesh(mesh.devices.reshape(4, 4, 8, 2), ("y", "x", "z", "c"))
    dp, tile = ("y", "x"), ("z", "c")
    placed = (
        P(dp, tile),
        P(dp, tile),
        P(tile, None, None, None),
        P(tile, None, None, None),
        P(tile, None),
        P(tile, None),
        P(tile),
    )
    return jax.shard_map(
        body,
        mesh=grid,
        in_specs=placed,
        out_specs=(P(dp, tile), P(dp, tile), P(tile, dp, None, None), P(tile, dp, None, None)),
        check_vma=False,
    )
```

```python
import functools

import jax
import jax.numpy as jnp
from jax import lax
from jax.experimental import pallas as pl
from jax.experimental.pallas import tpu as pltpu
from jax.sharding import Mesh, PartitionSpec as P

SIDE = 128
COLS = 32
ROWS = 8
VM = pltpu.VMEM
SM = pltpu.SMEM
BF = jnp.bfloat16
F32 = jnp.float32


def whole(*shape):
    return pl.BlockSpec(shape, lambda *i: (0,) * len(shape))


def vspec():
    return pl.BlockSpec(memory_space=VM)


def params(mib):
    return pltpu.CompilerParams(vmem_limit_bytes=mib << 20)


def sspec():
    return pl.BlockSpec(memory_space=SM)


def nn(a, b):
    return jnp.dot(a, b, preferred_element_type=F32)


def nt(a, b):
    return lax.dot_general(a, b, (((1,), (1,)), ((), ())), preferred_element_type=F32)


def gelu_pair(pre):
    curve = lax.erf(pre * 0.7071067811865476)
    value = 0.5 * pre * (1.0 + curve)
    slope = 0.5 * (1.0 + curve) + pre * jnp.exp(-0.5 * pre * pre) * 0.3989422804014327
    return value, slope


def other_owner(k):
    z, c = lax.axis_index("z"), lax.axis_index("c")
    ahead = 2 * c - 1
    if k < 2:
        return z * 2 + (c if k == 0 else 1 - c)
    hop = (k - 2) // 4 + 1
    kind = (k - 2) % 4
    chip = z + hop * ahead if kind in (0, 2) else z - hop * ahead
    core = c if kind in (0, 3) else 1 - c
    return lax.rem(chip + 8, 8) * 2 + core


def split(code):
    return code // COLS, lax.rem(code, COLS)


def dense_kernel(up, where, count_ref, tiles_ref, out_ref, sem):
    count = count_ref[0]
    out_ref[...] = jnp.zeros_like(out_ref)

    def copy(s):
        row, col = (lanes(k, SIDE) for k in split(where[s]))
        at = (col, row) if up else (row, col)
        return pltpu.make_async_copy(tiles_ref.at[0, s], out_ref.at[at], sem)

    @pl.loop(0, count)
    def _(s):
        copy(s).start()

    @pl.loop(0, count)
    def _(s):
        copy(s).wait()


def dense(where, count, tiles, up):
    features, hidden = COLS * SIDE, ROWS * SIDE
    return pl.pallas_call(
        functools.partial(dense_kernel, up),
        in_specs=[sspec()] * 2 + [pl.BlockSpec(memory_space=pltpu.HBM)],
        out_specs=vspec(),
        out_shape=jax.ShapeDtypeStruct((features, hidden) if up else (hidden, features), BF),
        scratch_shapes=[pltpu.SemaphoreType.DMA],
        compiler_params=params(16),
        cost_estimate=pl.CostEstimate(flops=0, bytes_accessed=12 << 20, transcendentals=0),
        name="dense_up" if up else "dense_down",
    )(where, count, tiles)


def lanes(k, n):
    return pl.ds(pl.multiple_of(k * n, n), n)


EARLY = 10


def early_kernel(*refs):
    shards, (wu_ref, wd_ref, pre_ref, gh_ref, x_ref, dy_ref, sem) = refs[:EARLY], refs[EARLY:]
    fetch_shards(shards, range(EARLY), x_ref, dy_ref, sem)
    wide = 2 * SIDE
    for n in range(ROWS // 2):
        at = slice(n * wide, (n + 1) * wide)
        pre_ref[:, at], gh_ref[:, at] = products(range(EARLY), at, x_ref, dy_ref, wu_ref, wd_ref)


def fetch_shards(shards, which, x_ref, dy_ref, sem):
    copies = []
    for k in which:
        at = lanes(other_owner(k), 2 * SIDE)
        copies.append(pltpu.make_async_copy(shards[k].at[0], x_ref.at[:, at], sem))
        copies.append(pltpu.make_async_copy(shards[k].at[1], dy_ref.at[:, at], sem))
    for copy in copies:
        copy.start()
    for copy in copies:
        copy.wait()


def products(which, at, x_ref, dy_ref, wu_ref, wd_ref):
    pre, grad_hidden = 0.0, 0.0
    for k in which:
        features = lanes(other_owner(k), 2 * SIDE)
        pre = pre + nn(x_ref[:, features], wu_ref[features, at])
        grad_hidden = grad_hidden + nt(dy_ref[:, features], wd_ref[at, features])
    return pre, grad_hidden


def early(shards, wu, wd):
    acc = jax.ShapeDtypeStruct((SIDE, ROWS * SIDE), F32)
    return pl.pallas_call(
        early_kernel,
        in_specs=[pl.BlockSpec(memory_space=pl.ANY)] * EARLY + [vspec()] * 2,
        out_specs=[vspec()] * 2,
        out_shape=[acc, acc],
        scratch_shapes=[VM((SIDE, COLS * SIDE), BF)] * 2 + [pltpu.SemaphoreType.DMA],
        compiler_params=params(16),
        cost_estimate=pl.CostEstimate(flops=5 << 28, bytes_accessed=13 << 20, transcendentals=0),
        name="early",
    )(*shards[:EARLY], wu, wd)


def forward_kernel(where, *refs):
    shards = refs[:16]
    wu_ref, wd_ref, pre_ref, gh_ref = refs[16:20]
    h_ref, d_ref, x_ref, dy_ref, dt_ref, ht_ref = refs[20:26]
    parts, sem = refs[26:28], refs[28]
    wide = 2 * SIDE
    fetch_shards(shards, range(16), x_ref, dy_ref, sem)
    for n in range(ROWS // 2):
        at = slice(n * wide, (n + 1) * wide)
        pre, grad_hidden = products(range(EARLY, 16), at, x_ref, dy_ref, wu_ref, wd_ref)
        value, slope = gelu_pair(pre + pre_ref[:, at])
        grad = (grad_hidden + gh_ref[:, at]) * slope
        h_ref[:, at] = value.astype(BF)
        d_ref[:, at] = grad.astype(BF)
        for b in range(2):
            half = slice(b * SIDE, (b + 1) * SIDE)
            ht_ref[2 * n + b] = value[:, half].T.astype(BF)
            dt_ref[2 * n + b] = grad[:, half].T.astype(BF)
    fill_parts(where, x_ref, dy_ref, dt_ref, ht_ref, parts, ((2, 0, 16), (2, 16, 16)))


def fill_parts(where, x_ref, dy_ref, dt_ref, ht_ref, outs, blocks):
    for out, (away, start, n) in zip(outs, blocks):
        for s in range(n):
            row, col = split(where[ring_slot(away, start + s)])
            at = lanes(col, SIDE)
            out[0, s] = nn(dt_ref[row], x_ref[:, at]).astype(BF)
            out[1, s] = nn(ht_ref[row], dy_ref[:, at]).astype(BF)


def forward(where, shards, wu, wd, first):
    hid = jax.ShapeDtypeStruct((SIDE, ROWS * SIDE), BF)
    tok = jax.ShapeDtypeStruct((SIDE, COLS * SIDE), BF)
    turned = jax.ShapeDtypeStruct((ROWS, SIDE, SIDE), BF)
    part = jax.ShapeDtypeStruct((2, 16, SIDE, SIDE), BF)
    return pl.pallas_call(
        forward_kernel,
        in_specs=[sspec()] + [pl.BlockSpec(memory_space=pl.ANY)] * 16 + [vspec()] * 4,
        out_specs=[vspec()] * 8,
        out_shape=[hid, hid, tok, tok, turned, turned, part, part],
        scratch_shapes=[pltpu.SemaphoreType.DMA],
        compiler_params=params(16),
        cost_estimate=pl.CostEstimate(flops=3 << 30, bytes_accessed=22 << 20, transcendentals=1 << 18),
        name="forward",
    )(where, *shards, wu, wd, *first)


REST = ((1, 16, 16), (3, 0, 16), (1, 0, 16), (3, 16, 16), (0, 0, 32))


def rest_kernel(where, x_ref, dy_ref, dt_ref, ht_ref, *outs):
    fill_parts(where, x_ref, dy_ref, dt_ref, ht_ref, outs, REST)


def rest_parts(where, x, dy, dt, ht):
    return pl.pallas_call(
        rest_kernel,
        in_specs=[sspec()] + [vspec()] * 4,
        out_specs=[vspec()] * len(REST),
        out_shape=[jax.ShapeDtypeStruct((2, n, SIDE, SIDE), BF) for _, _, n in REST],
        compiler_params=params(16),
        cost_estimate=pl.CostEstimate(flops=1 << 30, bytes_accessed=9 << 20, transcendentals=0),
        name="rest_parts",
    )(where, x, dy, dt, ht)


def ring_slot(away1, place):
    away2, near = ((2, 0), (1, 4), (2, 4), (3, 0), (1, 0), (3, 4), (0, 0), (0, 4))[place // 4]
    c = lax.axis_index("c")
    away_x = away1 + c * (away2 - away1)
    away_y = away2 + c * (away1 - away2)
    y = lax.rem(lax.axis_index("y") + away_y, 4)
    x = lax.rem(lax.axis_index("x") + away_x, 4)
    return (y * 4 + x) * 8 + near + place % 4


def token_kernel(h_ref, d_ref, wu_ref, wd_ref, send_ref, keep_ref):
    wide = 2 * SIDE
    c = lax.axis_index("c")
    for out, core in ((send_ref, 1 - c), (keep_ref, c)):
        for k in range(8):
            at = lanes(2 * k + core, wide)
            out[k, 0] = nn(h_ref[...], wd_ref[:, at]).astype(BF)
            out[k, 1] = nt(d_ref[...], wu_ref[at, :]).astype(BF)


def token_parts(h, d, wu, wd):
    part = jax.ShapeDtypeStruct((8, 2, SIDE, 2 * SIDE), BF)
    return pl.pallas_call(
        token_kernel,
        in_specs=[vspec()] * 4,
        out_specs=[vspec()] * 2,
        out_shape=[part] * 2,
        compiler_params=params(16),
        cost_estimate=pl.CostEstimate(flops=2 << 30, bytes_accessed=19 << 20, transcendentals=0),
        name="token_parts",
    )(h, d, wu, wd)


def ring(n, by):
    return [(i, (i + by) % n) for i in range(n)]


def step_both(x):
    pairs = []
    for z in range(8):
        pairs.append((z * 2, ((z + 1) % 8) * 2))
        pairs.append((z * 2 + 1, ((z - 1) % 8) * 2 + 1))
    return lax.ppermute(x, ("z", "c"), pairs)


def swap(x):
    return lax.ppermute(x, "c", [(0, 1), (1, 0)])


def add(*parts):
    total = parts[0].astype(F32)
    for p in parts[1:]:
        total = total + p.astype(F32)
    return total


def gather_over_tile(own, wu, wd):
    first, second = own, swap(own)
    shards = [first, second]
    for k in range(1, 5):
        if k == 3:
            first, wu = lax.optimization_barrier((first, wu))
        first = step_both(first)
        if k == 4:
            sums = early(shards, wu, wd)
            first, *sums = lax.optimization_barrier((first, *sums))
        shards += [first, swap(first)]
        if k == 3:
            second, wd = lax.optimization_barrier((second, wd))
        if k < 4:
            second = step_both(second)
            shards += [second, swap(second)]
    return shards, wu, wd, sums


def hop(t, stage, by):
    pairs = []
    for y in range(4):
        for x in range(4):
            for c in range(2):
                along_x = (stage + c) % 2 == 0
                to_y = y if along_x else (y + by) % 4
                to_x = (x + by) % 4 if along_x else x
                pairs.append(((y * 4 + x) * 2 + c, (to_y * 4 + to_x) * 2 + c))
    return lax.ppermute(t, ("y", "x", "c"), pairs)


def ring_sums(far_a, far_b, next_b, before_a, next_a, before_b, own, terms):
    from_left = hop(far_a, 0, 1)
    from_right = hop(far_b, 0, -1)
    left_b = hop(next_b, 0, 1)
    right_a = hop(before_a, 0, -1)
    left_a = hop(add(next_a, from_left).astype(BF), 0, 1)
    right_b = hop(add(before_b, from_right).astype(BF), 0, -1)
    left_a, left_b, right_a, right_b = lax.optimization_barrier((left_a, left_b, right_a, right_b))

    def total(k, n):
        left, right = (left_a, right_a) if k < 16 else (left_b, right_b)
        at = slice(k % 16, k % 16 + n)
        return add(own[:, k : k + n], left[:, at], right[:, at])

    from_left = hop(total(0, 8).astype(BF), 1, 1)
    from_right = hop(total(8, 8).astype(BF), 1, -1)
    from_left, terms = lax.optimization_barrier((from_left, terms))
    end_a = hop(add(total(16, 4), from_left[:, :4]).astype(BF), 1, 1)
    end_b = hop(add(total(20, 4), from_right[:, :4]).astype(BF), 1, -1)
    return (near_sum(own, left_b, right_b, from_left, from_right), end_a, end_b), terms


def near_sum_kernel(own, left_b, right_b, from_left, from_right, out):
    for k in range(2):
        for s in range(8):
            one = from_right[k, s] if s < 4 else from_left[k, s - 4]
            out[k, s] = add(own[k, s], left_b[k, s], right_b[k, s], one)


def near_sum(own, left_b, right_b, from_left, from_right):
    def last(block):
        return pl.BlockSpec((2, 8, SIDE, SIDE), lambda i: (0, block, 0, 0))

    half = pl.BlockSpec((2, 4, SIDE, SIDE), lambda i: (0, 1, 0, 0))
    return pl.pallas_call(
        near_sum_kernel,
        grid=(1,),
        in_specs=[last(3), last(1), last(1), half, half],
        out_specs=whole(2, 8, SIDE, SIDE),
        out_shape=jax.ShapeDtypeStruct((2, 8, SIDE, SIDE), F32),
        compiler_params=params(16),
        cost_estimate=pl.CostEstimate(flops=1 << 19, bytes_accessed=3 << 20, transcendentals=0),
        name="near_sum",
    )(own, left_b, right_b, from_left, from_right)


def finish_kernel(count_ref, near, end_a, end_b, up_out, down_out):
    first = lax.axis_index(("y", "x")) * 8
    for k in range(2):
        for s in range(8):
            total = add(near[k, s], end_a[k, s] if s < 4 else end_b[k, s - 4])
            total = jnp.where(first + s < count_ref[0], total * (1.0 / 16), 0.0)
            if k == 0:
                up_out[0, s] = total.T
            else:
                down_out[0, s] = total


def finish(count, sums):
    shape = (1, 8, SIDE, SIDE)
    return pl.pallas_call(
        finish_kernel,
        grid=(1,),
        in_specs=[sspec()] + [whole(2, n, SIDE, SIDE) for n in (8, 4, 4)],
        out_specs=[whole(*shape)] * 2,
        out_shape=[jax.ShapeDtypeStruct(shape, F32)] * 2,
        compiler_params=params(16),
        cost_estimate=pl.CostEstimate(flops=1 << 20, bytes_accessed=3 << 20, transcendentals=0),
        name="finish",
    )(count, *sums)


def owner_sum_kernel(terms_ref, mixed_ref, grad_in_ref):
    for k, out in enumerate((mixed_ref, grad_in_ref)):
        total = terms_ref[0, k].astype(F32)
        for z in range(1, 8):
            total = total + terms_ref[z, k].astype(F32)
        out[...] = total.astype(BF)


def owner_sum(terms):
    shape = terms.shape[2:]
    return pl.pallas_call(
        owner_sum_kernel,
        grid=(1,),
        in_specs=[whole(*terms.shape)],
        out_specs=[whole(*shape)] * 2,
        out_shape=[jax.ShapeDtypeStruct(shape, BF)] * 2,
        compiler_params=params(16),
        cost_estimate=pl.CostEstimate(flops=1 << 19, bytes_accessed=1 << 20, transcendentals=0),
        name="owner_sum",
    )(terms)


def body(tokens, grad_out, up_tiles, down_tiles, tile_rows, tile_cols, tile_count):
    where = tile_rows[0] * COLS + tile_cols[0]
    wu = dense(where, tile_count, up_tiles, True)
    wd = dense(where, tile_count, down_tiles, False)
    shards, wu, wd, first = gather_over_tile(jnp.stack([tokens, grad_out]), wu, wd)
    h, d, x, dy, dt, ht, *far = forward(where, shards, wu, wd, first)
    rest = rest_parts(where, x, dy, dt, ht)
    h, d, _ = lax.optimization_barrier((h, d, rest[0]))
    send, keep = token_parts(h, d, wu, wd)
    pieces = add(keep, swap(send)).astype(BF)
    terms = lax.all_to_all(pieces, "z", 0, 0, tiled=True)
    sums, terms = ring_sums(*far, *rest, terms)
    grad_up, grad_down = finish(tile_count, sums)
    mixed, grad_in = owner_sum(terms)
    return mixed, grad_in, grad_up, grad_down


def solution(mesh):
    grid = Mesh(mesh.devices.reshape(4, 4, 8, 2), ("y", "x", "z", "c"))
    dp, tile = ("y", "x"), ("z", "c")
    placed = (
        P(dp, tile),
        P(dp, tile),
        P(tile, None, None, None),
        P(tile, None, None, None),
        P(tile, None),
        P(tile, None),
        P(tile),
    )
    return jax.shard_map(
        body,
        mesh=grid,
        in_specs=placed,
        out_specs=(P(dp, tile), P(dp, tile), P(tile, dp, None, None), P(tile, dp, None, None)),
        check_vma=False,
    )
```
